128 devices in a mesh: leaf: 4 (over y_hi, core), front: 32 (over y_lo, z, x).
Axes of the slice: x: 4, y: 4 (y_hi: 2, y_lo: 2; y = y_hi * 2 + y_lo), z: 4, core: 2. Of those that a mesh axis runs over, the one named last changes fastest.
Arguments:
- leaf_source: float32 [4, 2048, 128], P('leaf', 'front'), may hold values from -6 to 6
- mid_source: float32 [4, 2048, 128], P('leaf', 'front'), may hold values from -6 to 6
- root_source: float32 [8192, 128], P('front'), may hold values from -6 to 6
- leaf_inverse: float32 [4, 2, 2048, 2048], P('leaf', None, 'front'), may hold values from -0.09375 to 0.09375
- leaf_coupling: float32 [4, 2, 4096, 2048], P('leaf', None, None, 'front'), may hold values from -0.09375 to 0.09375
- mid_inverse: float32 [4, 2, 2048, 4096], P('leaf', None, None, 'front'), may hold values from -0.0625 to 0.0625
- mid_coupling: float32 [4, 2, 8192, 2048], P('leaf', None, None, 'front'), may hold values from -0.0625 to 0.0625
- root_inverse: float32 [2, 8192, 8192], P(None, 'leaf', 'front'), may hold values from -0.046875 to 0.046875
- leaf_blocks: int32 [4, 32], P('leaf'), may hold values from 0 to 31, as said below
- mid_blocks: int32 [2, 64], replicated, may hold values from 0 to 63, as said below
Outputs:
- leaf_solution: float32 [4, 2048, 128], P('leaf', 'front')
- mid_solution: float32 [4, 2048, 128], P('leaf', 'front')
- root_solution: float32 [8192, 128], P('front')
The draws below stay inside these ranges and needn't reach their ends.
Inputs may be any that keep to these rules, and one draw needn't show every extreme that they name: `leaf_blocks`: each row holds every block number of a level-1 separator exactly once. `mid_blocks`: each row holds every block number of the root separator exactly once.
All inputs are finite; a program needn't handle non-finite values.
Results may differ from the reference program's by a relative error of at most 0.00015.
Values sent between devices are 32-bit elements; how exact they have to be, the bound alone decides.
A program may use at most 128 MiB of HBM per device.

```python
import jax
import jax.numpy as jnp
from jax import lax

S2 = 2048
S1 = 4096
S0 = 8192
NR = 64
N_LEAF = 4
N_FRONT = 32


def draw_leaf_blocks(key, part):
    rows = [jax.random.permutation(jax.random.fold_in(key, 101 + r), jnp.arange(S1 // 128, dtype=jnp.int32)) for r in range(N_LEAF)]
    return jnp.stack(rows).astype(jnp.int32)


def draw_mid_blocks(key, part):
    rows = [jax.random.permutation(jax.random.fold_in(key, 211 + r), jnp.arange(S0 // 128, dtype=jnp.int32)) for r in range(2)]
    return jnp.stack(rows).astype(jnp.int32)


def level_of(stream_key, extent, shards, least, high):
    gain, own = 1.0, jax.random.fold_in(stream_key, 6)
    for dim, shards_of in shards:
        steps = jnp.exp(jax.random.uniform(jax.random.fold_in(own, dim), (shards_of,), jnp.float32, least / len(shards), high / len(shards)))
        gain = gain * jnp.repeat(steps, extent[dim] // shards_of).reshape([-1 if axis == dim else 1 for axis in range(len(extent))])
    return gain


def gaussian(stream_key, extent, deviation, reach, shards=(), held_as=jnp.bfloat16):
    result = jax.random.normal(stream_key, extent, jnp.float32) * deviation
    if len(shards) > 0:
        result = level_of(stream_key, extent, shards, -0.22, 0.18) * result
    return jnp.clip(result, min=-reach, max=reach).astype(held_as)


def setup_inputs(seed: int = 0) -> dict:
    streams_of = jax.random.split(jax.random.key(seed), 11)
    leaf_source = gaussian(streams_of[0], (N_LEAF, S2, 2 * NR), 1.0, 6.0, ((0, 4), (1, 32)), jnp.float32)
    mid_source = gaussian(streams_of[1], (N_LEAF, S1 // 2, 2 * NR), 1.0, 6.0, ((0, 4), (1, 32)), jnp.float32)
    root_source = gaussian(streams_of[2], (S0, 2 * NR), 1.0, 6.0, ((0, 32),), jnp.float32)
    leaf_inverse = gaussian(streams_of[3], (N_LEAF, 2, S2, S2), (2 * S2) ** -0.5, 0.09375, ((0, 4), (2, 32)), jnp.float32)
    leaf_coupling = gaussian(streams_of[4], (N_LEAF, 2, S1, S2), (2 * S2) ** -0.5, 0.09375, ((0, 4), (3, 32)), jnp.float32)
    mid_inverse = gaussian(streams_of[5], (N_LEAF, 2, S1 // 2, S1), (2 * S1) ** -0.5, 0.0625, ((0, 4), (3, 32)), jnp.float32)
    mid_coupling = gaussian(streams_of[6], (N_LEAF, 2, S0, S1 // 2), (2 * S1) ** -0.5, 0.0625, ((0, 4), (3, 32)), jnp.float32)
    root_inverse = gaussian(streams_of[7], (2, S0, S0), (2 * S0) ** -0.5, 0.046875, ((1, 4), (2, 32)), jnp.float32)
    leaf_blocks = draw_leaf_blocks(jax.random.fold_in(streams_of[10], 71), 0)
    mid_blocks = draw_mid_blocks(jax.random.fold_in(streams_of[10], 71), 0)
    return {"leaf_source": leaf_source, "mid_source": mid_source, "root_source": root_source, "leaf_inverse": leaf_inverse, "leaf_coupling": leaf_coupling, "mid_inverse": mid_inverse, "mid_coupling": mid_coupling, "root_inverse": root_inverse, "leaf_blocks": leaf_blocks, "mid_blocks": mid_blocks}


exact_precision = lax.Precision.HIGHEST


def complex_apply(matrix, vectors):
    width = vectors.shape[1] // 2
    real_part = jnp.dot(matrix[0], vectors, precision=exact_precision, preferred_element_type=jnp.float32)
    imag_part = jnp.dot(matrix[1], vectors, precision=exact_precision, preferred_element_type=jnp.float32)
    return jnp.concatenate([real_part[:, :width] - imag_part[:, width:], real_part[:, width:] + imag_part[:, :width]], axis=1)


def complex_transposed(matrix, vectors):
    width = vectors.shape[1] // 2
    dims = (((0,), (0,)), ((), ()))
    real_part = lax.dot_general(matrix[0], vectors, dims, precision=exact_precision, preferred_element_type=jnp.float32)
    imag_part = lax.dot_general(matrix[1], vectors, dims, precision=exact_precision, preferred_element_type=jnp.float32)
    return jnp.concatenate([real_part[:, :width] - imag_part[:, width:], real_part[:, width:] + imag_part[:, :width]], axis=1)


def to_parent(values, blocks):
    inverse_order = jnp.argsort(blocks)
    count = values.shape[0] // 128
    return values.reshape(count, 128, values.shape[1])[inverse_order].reshape(values.shape)


def to_child(values, blocks):
    count = values.shape[0] // 128
    return values.reshape(count, 128, values.shape[1])[blocks].reshape(values.shape)


def reference(leaf_source, mid_source, root_source, leaf_inverse, leaf_coupling, mid_inverse, mid_coupling, root_inverse, leaf_blocks, mid_blocks):
    width2 = leaf_source.shape[2]
    half_rows = S1 // N_FRONT // 2
    solved_two = [complex_apply(leaf_inverse[c], leaf_source[c]) for c in range(N_LEAF)]
    mid_factor = []
    mid_couple = []
    solved_one = []
    for front_id in range(2):
        factor = jnp.concatenate([mid_inverse[2 * front_id], mid_inverse[2 * front_id + 1]], axis=1)
        couple = jnp.concatenate([mid_coupling[2 * front_id], mid_coupling[2 * front_id + 1]], axis=2)
        pair = mid_source[2 * front_id:2 * front_id + 2].reshape(2, N_FRONT, half_rows, width2)
        source_one = jnp.transpose(pair, (1, 0, 2, 3)).reshape(S1, width2)
        for child in (2 * front_id, 2 * front_id + 1):
            source_one = source_one - to_parent(complex_apply(leaf_coupling[child], solved_two[child]), leaf_blocks[child])
        mid_factor.append(factor)
        mid_couple.append(couple)
        solved_one.append(complex_apply(factor, source_one))
    reduced_root = root_source
    for front_id in range(2):
        reduced_root = reduced_root - to_parent(complex_apply(mid_couple[front_id], solved_one[front_id]), mid_blocks[front_id])
    solved_root = complex_apply(root_inverse, reduced_root)
    root_solution = complex_transposed(root_inverse, solved_root)
    mid_full = []
    mid_pieces = []
    for front_id in range(2):
        rest = solved_one[front_id] - complex_transposed(mid_couple[front_id], to_child(root_solution, mid_blocks[front_id]))
        solution_one = complex_transposed(mid_factor[front_id], rest)
        mid_full.append(solution_one)
        split = jnp.transpose(solution_one.reshape(N_FRONT, 2, half_rows, width2), (1, 0, 2, 3)).reshape(2, S1 // 2, width2)
        mid_pieces.append(split)
    mid_solution = jnp.concatenate(mid_pieces, axis=0)
    leaf_out = []
    for child in range(N_LEAF):
        rest = solved_two[child] - complex_transposed(leaf_coupling[child], to_child(mid_full[child // 2], leaf_blocks[child]))
        leaf_out.append(complex_transposed(leaf_inverse[child], rest))
    leaf_solution = jnp.stack(leaf_out, axis=0)
    return leaf_solution, mid_solution, root_solution
```

```python
import jax
import jax.numpy as jnp
from jax import lax
from jax.experimental import pallas as pl
from jax.experimental.pallas import tpu as pltpu
from jax.sharding import PartitionSpec as P

MESH = pl.DeviceIdType.MESH
F32 = jnp.float32
BF16 = jnp.bfloat16
NF = 32


def halves(x):
    hi = x.astype(BF16)
    lo = (x - hi.astype(F32)).astype(BF16)
    return hi, lo


def packed(x):
    return jnp.concatenate(halves(x), axis=1)


def turn(x):
    swapped = pltpu.roll(x, 64, 1)
    lane = lax.broadcasted_iota(jnp.int32, x.shape, 1)
    return jnp.where(lane < 64, -swapped, swapped)


def stacked(x):
    both = jnp.concatenate([packed(x), packed(turn(x))], axis=0)
    return jnp.concatenate([both, both], axis=0)


def dot(a, b):
    return jnp.dot(a, b, preferred_element_type=F32)


def fold(a):
    return a[:, :128] + a[:, 128:]


def combine(a, n):
    folded = fold(a)
    real = folded[:n] + folded[2 * n : 3 * n]
    imag = folded[n : 2 * n] + folded[3 * n :]
    return real + turn(imag)


def kernel(
    inv_two, inv_one, leaf_src, mid_src, root_src, leaf_inv, leaf_cpl, mid_inv, mid_cpl, root_inv,
    leaf_out, mid_out, root_out,
    st_l, st_c, st_m, st_k, st_r,
    lb, lt, cb, ct, mf, mt, kb, kt, rf, rt,
    ra, rb, rk, gx, gk, send, obuf, xbuf, xred, ybuf, xroot, zbuf, zsum, mx, acc, solved2, solved1,
    ld, ss, rs, xs_s, xs_r, gk_r, gk_fs, gk_fr, gx_r, gx_fs, gx_fr,
):
    leaf = lax.axis_index("leaf")
    me = lax.axis_index("front")
    h = lax.rem(leaf, 2)
    level = lax.div(leaf, 2)
    partner = (leaf + 1 - 2 * h, me)
    across = (lax.rem(leaf + 2, 4), me)

    def rcopy(src, dst, s, r, dev):
        return pltpu.make_async_remote_copy(
            src_ref=src, dst_ref=dst, send_sem=s, recv_sem=r, device_id=dev, device_id_type=MESH
        )

    def load_columns(src, dst, sem):
        def step(b, c):
            cols = pl.ds(pl.multiple_of(b * 128, 128), 128)
            pltpu.make_async_copy(src.at[:, :, cols], dst.at[b], sem).start()
            return c

        lax.fori_loop(0, dst.shape[0], step, 0)

    def loaded(dst, sem):
        pltpu.make_async_copy(dst, dst, sem).wait()

    load_columns(leaf_inv, st_l, ld.at[0])
    load_columns(leaf_cpl, st_c, ld.at[1])
    pltpu.make_async_copy(mid_inv, st_m, ld.at[2]).start()
    load_columns(mid_cpl, st_k, ld.at[3])
    pltpu.make_async_copy(root_inv, st_r, ld.at[4]).start()

    barrier = pltpu.get_barrier_semaphore()

    def greet(d, c):
        pl.semaphore_signal(barrier, 1, device_id=(leaf, lax.rem(me + d, NF)), device_id_type=MESH)
        return c

    lax.fori_loop(1, NF, greet, 0)
    pl.semaphore_signal(barrier, 1, device_id=partner, device_id_type=MESH)
    pl.semaphore_signal(barrier, 1, device_id=across, device_id_type=MESH)
    pl.semaphore_wait(barrier, NF + 1)

    def send_all(src, dst, ph):
        def step(d, c):
            rcopy(src, dst, ss.at[ph], rs.at[ph], (leaf, lax.rem(me + d, NF))).start()
            return c

        lax.fori_loop(1, NF, step, 0)

    def all_sent(buf, ph):
        some = buf.at[pl.ds(0, NF - 1)]
        rcopy(some, some, ss.at[ph], rs.at[ph], partner).wait_send()

    def all_here(buf, ph):
        some = buf.at[pl.ds(0, NF - 1)]
        rcopy(some, some, ss.at[ph], rs.at[ph], partner).wait_recv()

    def split_columns(st, b_ref, t_ref):
        def step(b, c):
            t = st[b].reshape(128, 128)
            hi, lo = halves(t)
            b_ref[b, 0:128, :] = hi
            b_ref[b, 128:256, :] = lo
            hi, lo = halves(t.T)
            t_ref[b, :, 0:128] = hi
            t_ref[b, :, 128:256] = lo
            return c

        lax.fori_loop(0, st.shape[0], step, 0)

    def split_rows(st, f_ref, t_ref, n):
        def step(b, c):
            rows = pl.ds(pl.multiple_of(b * 128, 128), 128)
            for part in range(2):
                t = st[part, rows, :]
                hi, lo = halves(t)
                f_ref[b, :, part * n : (part + 1) * n] = hi
                f_ref[b, :, (2 + part) * n : (3 + part) * n] = lo
                hi, lo = halves(t.T)
                t_ref[b, part * n : (part + 1) * n, :] = hi
                t_ref[b, (2 + part) * n : (3 + part) * n, :] = lo
            return c

        lax.fori_loop(0, 16, step, 0)

    ra[me] = leaf_src[...]
    send_all(leaf_src, ra.at[me], 0)
    loaded(st_l, ld.at[0])
    split_columns(st_l, lb, lt)
    loaded(st_c, ld.at[1])
    split_columns(st_c, cb, ct)
    all_here(ra, 0)
    lhs = jnp.concatenate([lb[b] for b in range(16)], axis=1)
    x = combine(dot(lhs, packed(ra[...].reshape(2048, 128))), 64)
    solved2[...] = x

    def lift(x, t_ref, block_of, o_ref, x_ref, r_ref, per, ph):
        half = o_ref.shape[2]
        groups = NF // per
        rhs = stacked(x)

        def start(g):
            return per * lax.rem(lax.div(me, per) + 1 + g, groups)

        def exchange(g):
            rows = pl.ds(start(g), per)
            return rcopy(o_ref.at[rows, 1 - h], x_ref.at[rows], xs_s.at[g], xs_r.at[g], partner)

        def finish(g):
            exchange(g).wait_recv()
            for i in range(per):
                j = start(g) + i
                o_ref[j, h] = o_ref[j, h] + x_ref[j]

                @pl.when(j != me)
                def _():
                    rcopy(o_ref.at[j, h], r_ref.at[me], ss.at[ph], rs.at[ph], (leaf, j)).start()

                @pl.when(j == me)
                def _():
                    r_ref[j] = o_ref[j, h]

        def step(g, c):
            j = start(g)
            lhs = jnp.concatenate([t_ref[block_of(j, i)] for i in range(4)], axis=0)
            out = fold(dot(lhs, rhs))
            o_ref[pl.ds(j, per)] = out.reshape(per, 2, half, 128)
            exchange(g).start()

            @pl.when(g > 0)
            def _():
                finish(g - 1)

            return c

        lax.fori_loop(0, groups, step, 0)
        finish(groups - 1)

        def done(g, c):
            exchange(g).wait_send()
            return c

        lax.fori_loop(0, groups, done, 0)

    obuf2 = obuf.at[:, :, pl.ds(0, 64)]
    xbuf2 = xbuf.at[:, pl.ds(0, 64)]
    lift(x, ct, lambda j, i: inv_two[0, j + i], obuf2, xbuf2, rb, 4, 1)
    loaded(st_m, ld.at[2])
    split_rows(st_m, mf, mt, 128)
    all_here(rb, 1)
    xred[h] = mid_src[...] - jnp.sum(rb[...], axis=0)
    swap = rcopy(xred.at[h], xred.at[h], ss.at[10], rs.at[10], partner)
    swap.start()
    swap.wait()
    x = xred[...].reshape(128, 128)

    def apply(x, f_ref, r_ref, ph):
        rhs = stacked(x)

        def step(g, c):
            j = 4 * lax.rem(lax.div(me, 4) + 1 + g, 8)
            b = lax.div(j, 2)
            lhs = jnp.concatenate([f_ref[b], f_ref[b + 1]], axis=0)
            send[pl.ds(j, 4)] = fold(dot(lhs, rhs)).reshape(4, 64, 128)
            for i in range(4):

                @pl.when(j + i != me)
                def _():
                    rcopy(send.at[j + i], r_ref.at[me], ss.at[ph], rs.at[ph], (leaf, j + i)).start()

            return c

        lax.fori_loop(0, 8, step, 0)
        r_ref[me] = send[me]

    all_sent(ra, 0)
    apply(x, mf, ra, 2)
    all_sent(rb, 1)
    loaded(st_k, ld.at[3])
    split_columns(st_k, kb, kt)
    all_here(ra, 2)
    x = jnp.sum(ra[...], axis=0)
    solved1[...] = x

    lift(x, kt, lambda j, i: inv_one[level, 2 * j + i], obuf, xbuf, rk, 2, 3)
    loaded(st_r, ld.at[4])
    split_rows(st_r, rf, rt, 256)
    all_here(rk, 3)
    ybuf[0] = jnp.sum(rk[...], axis=0)
    swap = rcopy(ybuf.at[0], ybuf.at[1], ss.at[11], rs.at[11], across)
    swap.start()
    swap.wait()
    rows = pl.ds(pl.multiple_of(h * 128, 128), 128)
    xroot[h] = root_src[rows, :] - (ybuf[0] + ybuf[1])
    swap = rcopy(xroot.at[h], xroot.at[h], ss.at[12], rs.at[12], partner)
    swap.start()
    swap.wait()
    x = xroot[...].reshape(256, 128)

    all_sent(ra, 2)
    apply(x, rf, rb, 4)
    all_here(rb, 4)
    gx1 = gx.at[:, 0]
    gx1[me] = jnp.sum(rb[...], axis=0)
    send_all(gx1.at[me], gx1.at[me], 5)
    all_here(gx1, 5)
    rhs = packed(gx1[...].reshape(2048, 128))

    for m in range(2):
        part = []
        for b in range(16):
            part.append(rt[b, m * 512 : (m + 1) * 512, :])
        acc[m * 512 : (m + 1) * 512, :] = dot(jnp.concatenate(part, axis=1), rhs)
    x = combine(acc[...], 256)
    zbuf[...] = x.reshape(2, 128, 128)
    swap = rcopy(zbuf.at[1 - h], zsum.at[0], ss.at[13], rs.at[13], partner)
    swap.start()
    swap.wait()
    zsum[1] = zbuf[h] + zsum[0]
    swap = rcopy(zsum.at[1], zsum.at[2], ss.at[14], rs.at[14], across)
    swap.start()
    swap.wait()
    gk[me, h] = zsum[1] + zsum[2]

    def gather(g_ref, r, fs, fr, ph, use, groups, per):
        def step(d, c):
            rcopy(g_ref.at[me, h], g_ref.at[me, h], ss.at[ph], r.at[me], (leaf, lax.rem(me + d, NF))).start()
            return c

        lax.fori_loop(1, NF, step, 0)

        def forward(j):
            return rcopy(g_ref.at[j, h], g_ref.at[j, h], fs.at[j], fr.at[j], partner)

        def other(j):
            return rcopy(g_ref.at[j, 1 - h], g_ref.at[j, 1 - h], fs.at[j], fr.at[j], partner)

        def source(g, i):
            return lax.rem(me + NF - (g * per + i), NF)

        def arrive(g):
            for i in range(per):
                j = source(g, i)

                @pl.when(j != me)
                def _():
                    rcopy(g_ref.at[j, h], g_ref.at[j, h], ss.at[ph], r.at[j], partner).wait_recv()

                forward(j).start()

        def consume(g):
            for i in range(per):
                other(source(g, i)).wait_recv()
            use(g, [source(g, i) for i in range(per)])

        def loop(g, c):
            arrive(g)

            @pl.when(g > 0)
            def _():
                consume(g - 1)

            return c

        lax.fori_loop(0, groups, loop, 0)
        consume(groups - 1)

        def done(j, c):
            forward(j).wait_send()
            return c

        lax.fori_loop(0, NF, done, 0)

    acc[0:256, :] = jnp.zeros((256, 256), F32)

    def use_root(g, js):
        lhs = jnp.concatenate([kb[inv_one[level, 2 * j + i]] for j in js for i in range(2)], axis=1)
        rhs = jnp.concatenate([packed(gk[j].reshape(256, 128)) for j in js], axis=0)
        acc[0:256, :] += dot(lhs, rhs)

    gather(gk, gk_r, gk_fs, gk_fr, 6, use_root, 8, 4)
    root_out[...] = gk[me].reshape(256, 128)
    x = solved1[...] - combine(acc[0:256, :], 64)

    ra[me] = x
    send_all(ra.at[me], ra.at[me], 7)
    all_here(ra, 7)
    rhs = packed(ra[...].reshape(2048, 128))
    x = combine(dot(jnp.concatenate([mt[b] for b in range(16)], axis=1), rhs), 128)
    mx[0:2] = x.reshape(2, 64, 128)
    all_sent(gx1, 5)
    swap = rcopy(mx.at[1 - h], mx.at[2], ss.at[15], rs.at[15], partner)
    swap.start()
    swap.wait()
    gx[me, h] = mx[h] + mx[2]
    mid_out[...] = gx[me, h]

    acc[0:256, :] = jnp.zeros((256, 256), F32)

    def use_mid(g, js):
        lhs = jnp.concatenate([cb[inv_two[0, j]] for j in js], axis=1)
        rhs = jnp.concatenate([packed(gx[j].reshape(128, 128)) for j in js], axis=0)
        acc[0:256, :] += dot(lhs, rhs)

    gather(gx, gx_r, gx_fs, gx_fr, 8, use_mid, 4, 8)
    x = solved2[...] - combine(acc[0:256, :], 64)

    all_sent(rb, 4)
    rhs = stacked(x)

    def last(g, c):
        j = 4 * lax.rem(lax.div(me, 4) + 1 + g, 8)
        b = lax.div(j, 2)
        lhs = jnp.concatenate([lt[b], lt[b + 1]], axis=0)
        send[pl.ds(j, 4)] = fold(dot(lhs, rhs)).reshape(4, 64, 128)
        for i in range(4):

            @pl.when(j + i != me)
            def _():
                rcopy(send.at[j + i], rb.at[me], ss.at[9], rs.at[9], (leaf, j + i)).start()

        return c

    lax.fori_loop(0, 8, last, 0)
    rb[me] = send[me]
    all_here(rb, 9)
    leaf_out[...] = jnp.sum(rb[...], axis=0)
    all_sent(rk, 3)
    all_sent(gk.at[:, 0], 6)
    all_sent(ra, 7)
    all_sent(gx1, 8)
    all_sent(rb, 9)


def inverse_order(blocks):
    count = blocks.shape[1]
    ids = jnp.arange(count, dtype=jnp.int32)
    hit = blocks[:, :, None] == ids[None, None, :]
    return jnp.sum(jnp.where(hit, ids[None, :, None], 0), axis=1)


def body(
    leaf_source, mid_source, root_source, leaf_inverse, leaf_coupling, mid_inverse, mid_coupling,
    root_inverse, leaf_blocks, mid_blocks,
):
    vmem = pl.BlockSpec(memory_space=pltpu.VMEM)
    smem = pl.BlockSpec(memory_space=pltpu.SMEM)
    hbm = pl.BlockSpec(memory_space=pl.ANY)
    v = pltpu.VMEM
    dma = pltpu.SemaphoreType.DMA
    leaf_out, mid_out, root_out = pl.pallas_call(
        kernel,
        out_shape=(
            jax.ShapeDtypeStruct((64, 128), F32),
            jax.ShapeDtypeStruct((64, 128), F32),
            jax.ShapeDtypeStruct((256, 128), F32),
        ),
        in_specs=[smem, smem, vmem, vmem, vmem, hbm, hbm, hbm, hbm, hbm],
        out_specs=(vmem, vmem, vmem),
        scratch_shapes=[
            v((16, 2, 64, 128), F32), v((32, 2, 64, 128), F32), v((2, 2048, 128), F32),
            v((64, 2, 64, 128), F32), v((2, 2048, 256), F32),
            v((16, 256, 128), BF16), v((16, 128, 256), BF16),
            v((32, 256, 128), BF16), v((32, 128, 256), BF16),
            v((16, 128, 512), BF16), v((16, 512, 128), BF16),
            v((64, 256, 128), BF16), v((64, 128, 256), BF16),
            v((16, 128, 1024), BF16), v((16, 1024, 128), BF16),
            v((32, 64, 128), F32), v((32, 64, 128), F32), v((32, 128, 128), F32),
            v((32, 2, 64, 128), F32), v((32, 2, 128, 128), F32),
            v((32, 64, 128), F32), v((32, 2, 128, 128), F32), v((32, 128, 128), F32),
            v((2, 64, 128), F32), v((2, 128, 128), F32), v((2, 128, 128), F32),
            v((2, 128, 128), F32), v((3, 128, 128), F32), v((3, 64, 128), F32),
            v((1024, 256), F32), v((64, 128), F32), v((64, 128), F32),
            dma((5,)), dma((16,)), dma((16,)), dma((16,)), dma((16,)),
            dma((32,)), dma((32,)), dma((32,)), dma((32,)), dma((32,)), dma((32,)),
        ],
        compiler_params=pltpu.CompilerParams(
            collective_id=0, has_side_effects=True, vmem_limit_bytes=67043328
        ),
    )(
        inverse_order(leaf_blocks), inverse_order(mid_blocks),
        leaf_source[0], mid_source[0], root_source,
        leaf_inverse[0], jnp.swapaxes(leaf_coupling[0], 1, 2), mid_inverse[0],
        jnp.swapaxes(mid_coupling[0], 1, 2), root_inverse,
    )
    return leaf_out[None], mid_out[None], root_out


def solution(mesh):
    placed = (
        P("leaf", "front", None), P("leaf", "front", None), P("front", None),
        P("leaf", None, "front", None), P("leaf", None, None, "front"),
        P("leaf", None, None, "front"), P("leaf", None, None, "front"),
        P(None, "leaf", "front"), P("leaf", None), P(),
    )
    return jax.shard_map(
        body,
        mesh=mesh,
        in_specs=placed,
        out_specs=(P("leaf", "front", None), P("leaf", "front", None), P("front", None)),
        check_vma=False,
    )
```

```python
import jax
import jax.numpy as jnp
from jax import lax
from jax.experimental import pallas as pl
from jax.experimental.pallas import tpu as pltpu
from jax.sharding import PartitionSpec as P

MESH = pl.DeviceIdType.MESH
F32 = jnp.float32
BF16 = jnp.bfloat16
NF = 32


def lanes(x):
    return lax.broadcasted_iota(jnp.int32, x.shape, x.ndim - 1)


def low(x):
    return lanes(x) < 64


def quarter(x):
    return lanes(x) // 32


def pick(x, batch):
    x = pltpu.roll(x, 96, 1) if batch else x
    q = quarter(x)
    upper = jnp.where(q == 2, pltpu.roll(x, 64, 1), pltpu.roll(x, 32, 1))
    return jnp.where(q == 0, x, jnp.where(q == 1, pltpu.roll(x, 96, 1), upper))


def join(a, b):
    q = quarter(a)
    upper = jnp.where(q == 2, pltpu.roll(a, 32, 1), b)
    return jnp.where(q == 0, a, jnp.where(q == 1, pltpu.roll(b, 32, 1), upper))


def squeeze(wide):
    n = wide.shape[0] // 64
    parts = wide.reshape(n, 2, 32, 128)
    first, second = parts[:, 0], parts[:, 1]
    return jnp.where(low(first), first, second).reshape(n * 32, 128)


def spread(packed):
    n = packed.shape[0] // 32
    other = pltpu.roll(packed, 64, 1)
    first = jnp.where(low(packed), packed, other).reshape(n, 32, 128)
    second = jnp.where(low(packed), other, packed).reshape(n, 32, 128)
    return jnp.concatenate([first, second], axis=1).reshape(n * 64, 128)


def halves(x):
    hi = x.astype(BF16)
    lo = (x - hi.astype(F32)).astype(BF16)
    return hi, lo


def pair(wide):
    hi = wide.astype(BF16).astype(F32)
    return jnp.where(low(wide), hi, wide - hi).astype(BF16)


def turn(wide):
    swapped = pltpu.roll(wide, 32, 1)
    return jnp.where(lanes(wide) % 64 < 32, -swapped, swapped)


def stacked(wide):
    both = jnp.concatenate([pair(wide), pair(turn(wide))], axis=0)
    return jnp.concatenate([both, both], axis=0)


def dot(a, b):
    return jnp.dot(a, b, preferred_element_type=F32)


def fold(a):
    return a + pltpu.roll(a, 64, 1)


def combine(a, n):
    folded = fold(a)
    real = folded[:n] + folded[2 * n : 3 * n]
    imag = folded[n : 2 * n] + folded[3 * n :]
    return real + turn(imag)


def kernel(
    inv_two, inv_one, leaf_src, mid_src, root_src, leaf_inv, leaf_cpl, mid_inv, mid_cpl, root_inv,
    leaf_out, mid_out, root_out,
    st_l, st_c, st_m, st_k, st_r,
    lb, lt, cb, ct, mf, mt, kb, kt, rf, rt,
    g1_, g6_, g8_, gk_, gx_, send_, obuf_, xbuf_, in1_, in1k_, part_, in2_, in2k_,
    xred_, ybuf_, xroot_, zbuf_, zsum_, mx_, acc, solved2_, solved1_,
    ld, ss_, rs_, fs_, fr_,
):
    leaf = lax.axis_index("leaf")
    me = lax.axis_index("front")
    h = lax.rem(leaf, 2)
    level = lax.div(leaf, 2)
    partner = (leaf + 1 - 2 * h, me)
    across = (lax.rem(leaf + 2, 4), me)
    my_x = lax.rem(me, 4)
    my_z = lax.rem(lax.div(me, 4), 4)
    my_y = lax.div(me, 16)
    line = (my_z, my_x)
    spot = (my_y * 4 + my_x, my_y * 4 + my_z)

    def on_line(way, i):
        return (leaf, my_y * 16 + (i * 4 + my_x if way == 0 else my_z * 4 + i))

    def in_plane(way, u):
        y, other = lax.div(u, 4), lax.rem(u, 4)
        return (leaf, y * 16 + (my_z * 4 + other if way == 0 else other * 4 + my_x))

    def along(way, d):
        return lax.rem(line[way] + d, 4)

    def around(way, d):
        return lax.rem(spot[way] + d, 8)

    def rcopy(src, dst, s, r, dev):
        return pltpu.make_async_remote_copy(
            src_ref=src, dst_ref=dst, send_sem=s, recv_sem=r, device_id=dev, device_id_type=MESH
        )

    def load_columns(src, dst, sem):
        def step(b, c):
            cols = pl.ds(pl.multiple_of(b * 128, 128), 128)
            pltpu.make_async_copy(src.at[:, :, cols], dst.at[b], sem).start()
            return c

        lax.fori_loop(0, dst.shape[0], step, 0)

    def loaded(dst, sem):
        pltpu.make_async_copy(dst, dst, sem).wait()

    load_columns(leaf_inv, st_l, ld.at[0])
    load_columns(leaf_cpl, st_c, ld.at[1])
    pltpu.make_async_copy(mid_inv, st_m, ld.at[2]).start()
    load_columns(mid_cpl, st_k, ld.at[3])
    pltpu.make_async_copy(root_inv, st_r, ld.at[4]).start()

    barrier = pltpu.get_barrier_semaphore()

    def greet(dev):
        pl.semaphore_signal(barrier, 1, device_id=dev, device_id_type=MESH)

    for d in range(1, 8):
        greet(in_plane(0, around(0, d)))
        if d != 4:
            greet(in_plane(1, around(1, d)))
    greet(partner)
    greet(across)
    pl.semaphore_wait(barrier, 15)

    def split_columns(st, b_ref, t_ref):
        def step(b, c):
            t = st[b].reshape(128, 128)
            hi, lo = halves(t)
            b_ref[b, 0:128, :] = hi
            b_ref[b, 128:256, :] = lo
            hi, lo = halves(t.T)
            t_ref[b, :, 0:128] = hi
            t_ref[b, :, 128:256] = lo
            return c

        lax.fori_loop(0, st.shape[0], step, 0)

    def split_rows(st, f_ref, t_ref, n):
        def step(b, c):
            rows = pl.ds(pl.multiple_of(b * 128, 128), 128)
            for part in range(2):
                t = st[part, rows, :]
                hi, lo = halves(t)
                f_ref[b, :, part * n : (part + 1) * n] = hi
                f_ref[b, :, (2 + part) * n : (3 + part) * n] = lo
                hi, lo = halves(t.T)
                t_ref[b, part * n : (part + 1) * n, :] = hi
                t_ref[b, (2 + part) * n : (3 + part) * n, :] = lo
            return c

        lax.fori_loop(0, 16, step, 0)

    def chain(batch):
        g1, g6, g8, gk, gx = (r.at[batch] for r in (g1_, g6_, g8_, gk_, gx_))
        send, obuf, xbuf, in1, in1k = (r.at[batch] for r in (send_, obuf_, xbuf_, in1_, in1k_))
        part, xred, ybuf, xroot = (r.at[batch] for r in (part_, xred_, ybuf_, xroot_))
        zbuf, zsum, mx, in2k = (r.at[batch] for r in (zbuf_, zsum_, mx_, in2k_))
        solved2, solved1 = solved2_.at[batch], solved1_.at[batch]
        ss, rs, fs, fr = (r.at[batch] for r in (ss_, rs_, fs_, fr_))
        part16 = part.at[:, :, pl.ds(0, 16)]

        def wait_send(some, k):
            rcopy(some, some, ss.at[k], rs.at[k], partner).wait_send()

        def wait_recv(some, k):
            rcopy(some, some, ss.at[k], rs.at[k], partner).wait_recv()

        def three(buf, way):
            return buf.at[way, pl.ds(0, 3)]

        def seven(buf, way):
            return buf.at[way, pl.ds(0, 7)]

        def sum_send(way, d, out, into, k):
            to = along(way, d)
            rcopy(
                out.at[way, to], into.at[way, line[way]], ss.at[k + way], rs.at[k + way], on_line(way, to)
            ).start()

        def sum_own(out, into):
            for way in range(2):
                into[way, line[way]] = out[way, line[way]]

        def sum_second(into, part, into2, k):
            for way in range(2):
                wait_recv(three(into, way), k + way)
            for way in range(2):
                part[way] = jnp.sum(into[way], axis=0)
                into2[way, spot[way]] = part[way, spot[way]]
            for way in range(2):
                for d in range(1, 8):
                    u = around(way, d)
                    rcopy(
                        part.at[way, u], into2.at[way, spot[way]], ss.at[k + 2 + way], rs.at[k + 2 + way],
                        in_plane(way, u),
                    ).start()

        def sum_last(into2, k):
            for way in range(2):
                wait_recv(seven(into2, way), k + 2 + way)
            return jnp.concatenate([jnp.sum(into2[0], axis=0), jnp.sum(into2[1], axis=0)], axis=0)

        def sum_sent(into, into2, k):
            for way in range(2):
                wait_send(three(into, way), k + way)
                wait_send(seven(into2, way), k + 2 + way)

        def share_first(rows, g, k):
            n = rows.shape[0] // 2
            for way in range(2):
                g[way, line[way], spot[way]] = rows[way * n : (way + 1) * n]
                mine = g.at[way, line[way], spot[way]]
                for d in range(1, 8):
                    u = around(way, d)
                    rcopy(mine, mine, ss.at[k + way], rs.at[k + way], in_plane(way, u)).start()

        def share_second(g, k):
            for way in range(2):
                wait_recv(g.at[way, 0, pl.ds(0, 7)], k + way)
                mine = g.at[way, line[way]]
                for d in range(1, 4):
                    to = on_line(way, along(way, d))
                    rcopy(mine, mine, ss.at[k + 2 + way], rs.at[k + 2 + way], to).start()

        def share_last(g, k):
            for way in range(2):
                wait_recv(three(g, way), k + 2 + way)

        def share_sent(g, k):
            for way in range(2):
                wait_send(g.at[way, 0, pl.ds(0, 7)], k + way)
                wait_send(three(g, way), k + 2 + way)

        def rows_of(g):
            rows = []
            for j in range(NF):
                y, z, x = j // 16, j // 4 % 4, j % 4
                rows += [g[0, z, y * 4 + x], g[1, x, y * 4 + z]]
            return pair(spread(jnp.concatenate(rows, axis=0)))

        def lift_exchange(o_ref, x_ref, way, i, k):
            at = 4 * way + i
            return rcopy(o_ref.at[1 - h, way, i], x_ref.at[way, i], fs.at[k + at], fr.at[k + at], partner)

        def lift_start(x, t_ref, blocks_of, o_ref, x_ref, subs, k):
            rhs = stacked(x)
            n = o_ref.shape[4]
            wide = 8 // subs

            def step(d, c):
                z = along(0, d)

                def sub(s, c):
                    u = s * wide
                    y, x0 = lax.div(u, 4), lax.rem(u, 4)
                    j = y * 16 + z * 4 + x0
                    lhs = jnp.concatenate([t_ref[b] for b in blocks_of(j)], axis=0)
                    out = squeeze(fold(dot(lhs, rhs))).reshape(wide, 2, 2 * n, 128)
                    for i in range(wide):
                        for side in range(2):
                            o_ref[side, 0, z, u + i] = out[i, side, 0:n]
                            o_ref[side, 1, x0 + i, y * 4 + z] = out[i, side, n : 2 * n]
                    return c

                lax.fori_loop(0, subs, sub, 0)
                lift_exchange(o_ref, x_ref, 0, z, k).start()
                return c

            lax.fori_loop(1, 5, step, 0)
            for d in range(1, 5):
                lift_exchange(o_ref, x_ref, 1, along(1, d), k).start()

        def lift_send(o_ref, x_ref, into, k, phase):
            mine = o_ref.at[h]
            for way in range(2):
                for d in range(1, 5):
                    i = along(way, d)
                    lift_exchange(o_ref, x_ref, way, i, k).wait_recv()
                    mine[way, i] = mine[way, i] + x_ref[way, i]
                    if d < 4:
                        sum_send(way, d, mine, into, phase)
            sum_own(mine, into)
            for way in range(2):
                for i in range(4):
                    lift_exchange(o_ref, x_ref, way, i, k).wait_send()

        def apply(x, f_ref, into, phase):
            rhs = stacked(x)

            def step(d, c):
                z = along(0, d)
                lhs = jnp.concatenate([f_ref[8 * y + 2 * z + i] for y in range(2) for i in range(2)], axis=0)
                out = squeeze(fold(dot(lhs, rhs))).reshape(8, 32, 128)
                send[0, z] = out[:, 0:16]
                for u in range(8):
                    send[1, u % 4, u // 4 * 4 + z] = out[u, 16:32]

                @pl.when(d < 4)
                def _():
                    sum_send(0, d, send, into, phase)

                return c

            lax.fori_loop(1, 5, step, 0)
            for d in range(1, 4):
                sum_send(1, d, send, into, phase)
            sum_own(send, into)

        def forward(g_ref, side, way, i, k):
            at = k + 4 * way + i
            return rcopy(g_ref.at[side, way, i], g_ref.at[side, way, i], fs.at[at], fr.at[at], partner)

        def forward_own(g_ref, k):
            for way in range(2):
                forward(g_ref, h, way, line[way], k).start()

        def forward_rest(g_ref, k):
            for way in range(2):
                for d in range(1, 4):
                    forward(g_ref, h, way, along(way, d), k).start()

        def gather_use(g_ref, blocks_of, b_ref, k):
            for way in range(2):
                for i in range(4):
                    forward(g_ref, 1 - h, way, i, k).wait_recv()
            acc[0:256, :] = jnp.zeros((256, 128), F32)

            def step(z, c):
                lhs, rows = [], []
                for u in range(8):
                    y, x = u // 4, u % 4
                    lhs += [b_ref[b] for b in blocks_of(y * 16 + z * 4 + x)]
                    for side in range(2):
                        rows += [g_ref[side, 0, z, u], g_ref[side, 1, x, y * 4 + z]]
                rhs = pair(spread(jnp.concatenate(rows, axis=0)))
                acc[0:256, :] += dot(jnp.concatenate(lhs, axis=1), rhs)
                return c

            lax.fori_loop(0, 4, step, 0)
            for way in range(2):
                for i in range(4):
                    forward(g_ref, h, way, i, k).wait_send()
            return combine(acc[0:256, :], 64)

        def swap(src, dst, k, dev):
            copy = rcopy(src, dst, ss.at[k], rs.at[k], dev)
            copy.start()
            return copy

        share_first(squeeze(pick(leaf_src[...], batch)), g1, 0)
        yield
        share_second(g1, 0)
        yield
        share_last(g1, 0)
        lhs = jnp.concatenate([lb[b] for b in range(16)], axis=1)
        x = combine(dot(lhs, rows_of(g1)), 64)
        solved2[...] = x
        obuf2 = obuf.at[:, :, :, :, pl.ds(0, 16)]
        xbuf2 = xbuf.at[:, :, :, pl.ds(0, 16)]
        in2 = in2_.at[batch, 0]
        lift_start(x, ct, lambda j: [inv_two[0, j + i] for i in range(4)], obuf2, xbuf2, 2, 0)
        yield
        lift_send(obuf2, xbuf2, in1, 0, 4)
        yield
        sum_second(in1, part16, in2, 4)
        yield
        xred[h] = squeeze(pick(mid_src[...], batch)) - sum_last(in2, 4)
        copy = swap(xred.at[h], xred.at[h], 40, partner)
        yield
        copy.wait()
        in2 = in2_.at[batch, 1]
        apply(spread(xred[...].reshape(64, 128)), mf, in1, 8)
        yield
        sum_sent(in1, in2, 4)
        sum_second(in1, part16, in2, 8)
        yield
        x = spread(sum_last(in2, 8))
        solved1[...] = x
        lift_start(
            x, kt, lambda j: [inv_one[level, 2 * j + i] for i in range(4)], obuf, xbuf, 4, 8
        )
        yield
        lift_send(obuf, xbuf, in1k, 8, 12)
        yield
        sum_sent(in1, in2, 8)
        sum_second(in1k, part, in2k, 12)
        yield
        ybuf[0] = sum_last(in2k, 12)
        copy = swap(ybuf.at[0], ybuf.at[1], 41, across)
        yield
        copy.wait()
        rows = pl.ds(pl.multiple_of(h * 128, 128), 128)
        xroot[h] = squeeze(pick(root_src[rows, :], batch)) - (ybuf[0] + ybuf[1])
        copy = swap(xroot.at[h], xroot.at[h], 42, partner)
        yield
        copy.wait()
        in2 = in2_.at[batch, 2]
        apply(spread(xroot[...].reshape(128, 128)), rf, in1, 16)
        yield
        sum_sent(in1k, in2k, 12)
        sum_second(in1, part16, in2, 16)
        yield
        share_first(sum_last(in2, 16), g6, 20)
        yield
        share_second(g6, 20)
        yield
        share_last(g6, 20)
        rhs = rows_of(g6)
        for m in range(2):
            lhs = jnp.concatenate([rt[b, m * 512 : (m + 1) * 512, :] for b in range(16)], axis=1)
            acc[m * 512 : (m + 1) * 512, :] = dot(lhs, rhs)
        zbuf[...] = squeeze(combine(acc[...], 256)).reshape(2, 64, 128)
        copy = swap(zbuf.at[1 - h], zsum.at[0], 43, partner)
        yield
        copy.wait()
        zsum[1] = zbuf[h] + zsum[0]
        copy = swap(zsum.at[1], zsum.at[2], 44, across)
        yield
        copy.wait()
        share_first(zsum[1] + zsum[2], gk.at[h], 24)
        yield
        share_second(gk.at[h], 24)
        forward_own(gk, 16)
        yield
        share_last(gk.at[h], 24)
        forward_rest(gk, 16)
        yield
        pulled = gather_use(gk, lambda j: [inv_one[level, 2 * j], inv_one[level, 2 * j + 1]], kb, 16)
        share_first(squeeze(solved1[...] - pulled), g8, 28)
        yield
        share_second(g8, 28)
        yield
        share_last(g8, 28)
        lhs = jnp.concatenate([mt[b] for b in range(16)], axis=1)
        x = combine(dot(lhs, rows_of(g8)), 128)
        mx[0:2] = squeeze(x).reshape(2, 32, 128)
        copy = swap(mx.at[1 - h], mx.at[2], 45, partner)
        yield
        copy.wait()
        share_first(mx[h] + mx[2], gx.at[h], 32)
        yield
        share_second(gx.at[h], 32)
        forward_own(gx, 24)
        yield
        share_last(gx.at[h], 32)
        forward_rest(gx, 24)
        yield
        pulled = gather_use(gx, lambda j: [inv_two[0, j]], cb, 24)
        sum_sent(in1, in2, 16)
        in2 = in2_.at[batch, 3]
        apply(solved2[...] - pulled, lt, in1, 36)
        yield
        sum_second(in1, part16, in2, 36)
        yield
        solved2[...] = spread(sum_last(in2, 36))
        sum_sent(in1, in2, 36)
        share_sent(g1, 0)
        share_sent(g6, 20)
        share_sent(gk.at[h], 24)
        share_sent(g8, 28)
        share_sent(gx.at[h], 32)

    def prepare_leaf():
        loaded(st_l, ld.at[0])
        split_columns(st_l, lb, lt)
        loaded(st_c, ld.at[1])
        split_columns(st_c, cb, ct)

    def prepare_mid():
        loaded(st_m, ld.at[2])
        split_rows(st_m, mf, mt, 128)

    def prepare_mid_coupling():
        loaded(st_k, ld.at[3])
        split_columns(st_k, kb, kt)

    def prepare_root():
        loaded(st_r, ld.at[4])
        split_rows(st_r, rf, rt, 256)

    prepare = {0: prepare_leaf, 1: prepare_mid, 3: prepare_mid_coupling, 6: prepare_root}
    batches = [chain(0), chain(1)]
    running, at = True, 0
    while running:
        for solve in batches:
            running = next(solve, True) is None
        prepare.get(at, lambda: None)()
        at += 1
    leaf_out[...] = join(solved2_[0], solved2_[1])

    def own_rows(g):
        halves_of = []
        for side in range(2):
            halves_of += [g[side, way, line[way], spot[way]] for way in range(2)]
        return halves_of

    mid = [spread(jnp.concatenate([gx_[b, h, w, line[w], spot[w]] for w in range(2)], axis=0)) for b in range(2)]
    mid_out[...] = join(*mid)
    root_out[...] = join(*[spread(jnp.concatenate(own_rows(gk_.at[b]), axis=0)) for b in range(2)])


def inverse_order(blocks):
    count = blocks.shape[1]
    ids = jnp.arange(count, dtype=jnp.int32)
    hit = blocks[:, :, None] == ids[None, None, :]
    return jnp.sum(jnp.where(hit, ids[None, :, None], 0), axis=1)


def body(
    leaf_source, mid_source, root_source, leaf_inverse, leaf_coupling, mid_inverse, mid_coupling,
    root_inverse, leaf_blocks, mid_blocks,
):
    vmem = pl.BlockSpec(memory_space=pltpu.VMEM)
    smem = pl.BlockSpec(memory_space=pltpu.SMEM)
    hbm = pl.BlockSpec(memory_space=pl.ANY)
    v = pltpu.VMEM
    dma = pltpu.SemaphoreType.DMA
    leaf_out, mid_out, root_out = pl.pallas_call(
        kernel,
        out_shape=(
            jax.ShapeDtypeStruct((64, 128), F32),
            jax.ShapeDtypeStruct((64, 128), F32),
            jax.ShapeDtypeStruct((256, 128), F32),
        ),
        in_specs=[smem, smem, vmem, vmem, vmem, hbm, hbm, hbm, hbm, hbm],
        out_specs=(vmem, vmem, vmem),
        scratch_shapes=[
            v((16, 2, 64, 128), F32), v((32, 2, 64, 128), F32), v((2, 2048, 128), F32),
            v((64, 2, 64, 128), F32), v((2, 2048, 256), F32),
            v((16, 256, 128), BF16), v((16, 128, 256), BF16),
            v((32, 256, 128), BF16), v((32, 128, 256), BF16),
            v((16, 128, 512), BF16), v((16, 512, 128), BF16),
            v((64, 256, 128), BF16), v((64, 128, 256), BF16),
            v((16, 128, 1024), BF16), v((16, 1024, 128), BF16),
            v((2, 2, 4, 8, 16, 128), F32), v((2, 2, 4, 8, 16, 128), F32), v((2, 2, 4, 8, 16, 128), F32),
            v((2, 2, 2, 4, 8, 32, 128), F32), v((2, 2, 2, 4, 8, 16, 128), F32),
            v((2, 2, 4, 8, 16, 128), F32), v((2, 2, 2, 4, 8, 32, 128), F32), v((2, 2, 4, 8, 32, 128), F32),
            v((2, 2, 4, 8, 16, 128), F32), v((2, 2, 4, 8, 32, 128), F32), v((2, 2, 8, 32, 128), F32),
            v((2, 4, 2, 8, 16, 128), F32), v((2, 2, 8, 32, 128), F32),
            v((2, 2, 32, 128), F32), v((2, 2, 64, 128), F32), v((2, 2, 64, 128), F32),
            v((2, 2, 64, 128), F32), v((2, 3, 64, 128), F32), v((2, 3, 32, 128), F32),
            v((1024, 128), F32), v((2, 64, 128), F32), v((2, 64, 128), F32),
            dma((5,)), dma((2, 48)), dma((2, 48)), dma((2, 32)), dma((2, 32)),
        ],
        compiler_params=pltpu.CompilerParams(
            collective_id=0, has_side_effects=True, vmem_limit_bytes=67043328
        ),
    )(
        inverse_order(leaf_blocks), inverse_order(mid_blocks),
        leaf_source[0], mid_source[0], root_source,
        leaf_inverse[0], jnp.swapaxes(leaf_coupling[0], 1, 2), mid_inverse[0],
        jnp.swapaxes(mid_coupling[0], 1, 2), root_inverse,
    )
    return leaf_out[None], mid_out[None], root_out


def solution(mesh):
    placed = (
        P("leaf", "front", None), P("leaf", "front", None), P("front", None),
        P("leaf", None, "front", None), P("leaf", None, None, "front"),
        P("leaf", None, None, "front"), P("leaf", None, None, "front"),
        P(None, "leaf", "front"), P("leaf", None), P(),
    )
    return jax.shard_map(
        body,
        mesh=mesh,
        in_specs=placed,
        out_specs=(P("leaf", "front", None), P("leaf", "front", None), P("front", None)),
        check_vma=False,
    )
```

```python
import jax
import jax.numpy as jnp
from jax import lax
from jax.experimental import pallas as pl
from jax.experimental.pallas import tpu as pltpu
from jax.sharding import PartitionSpec as P

MESH = pl.DeviceIdType.MESH
F32 = jnp.float32
BF16 = jnp.bfloat16
NF = 32


def lanes(x):
    return lax.broadcasted_iota(jnp.int32, x.shape, x.ndim - 1)


def low(x):
    return lanes(x) < 64


def quarter(x):
    return lanes(x) // 32


def pick(x, batch):
    x = pltpu.roll(x, 96, 1) if batch else x
    q = quarter(x)
    upper = jnp.where(q == 2, pltpu.roll(x, 64, 1), pltpu.roll(x, 32, 1))
    return jnp.where(q == 0, x, jnp.where(q == 1, pltpu.roll(x, 96, 1), upper))


def join(a, b):
    q = quarter(a)
    upper = jnp.where(q == 2, pltpu.roll(a, 32, 1), b)
    return jnp.where(q == 0, a, jnp.where(q == 1, pltpu.roll(b, 32, 1), upper))


def squeeze(wide):
    n = wide.shape[0] // 64
    parts = wide.reshape(n, 2, 32, 128)
    first, second = parts[:, 0], parts[:, 1]
    return jnp.where(low(first), first, second).reshape(n * 32, 128)


def spread(packed):
    n = packed.shape[0] // 32
    other = pltpu.roll(packed, 64, 1)
    first = jnp.where(low(packed), packed, other).reshape(n, 32, 128)
    second = jnp.where(low(packed), other, packed).reshape(n, 32, 128)
    return jnp.concatenate([first, second], axis=1).reshape(n * 64, 128)


def halves(x):
    hi = x.astype(BF16)
    lo = (x - hi.astype(F32)).astype(BF16)
    return hi, lo


def pair(wide):
    hi = wide.astype(BF16).astype(F32)
    return jnp.where(low(wide), hi, wide - hi).astype(BF16)


def turn(wide):
    swapped = pltpu.roll(wide, 32, 1)
    return jnp.where(lanes(wide) % 64 < 32, -swapped, swapped)


def stacked(wide):
    both = jnp.concatenate([pair(wide), pair(turn(wide))], axis=0)
    return jnp.concatenate([both, both], axis=0)


def dot(a, b):
    return jnp.dot(a, b, preferred_element_type=F32)


def fold(a):
    return a + pltpu.roll(a, 64, 1)


def combine(a, n):
    folded = fold(a)
    real = folded[:n] + folded[2 * n : 3 * n]
    imag = folded[n : 2 * n] + folded[3 * n :]
    return real + turn(imag)


def kernel(
    inv_two, inv_one, leaf_src, mid_src, root_src, leaf_inv, leaf_cpl, mid_inv, mid_cpl, root_inv,
    leaf_out, mid_out, root_out,
    st_l, st_c, st_m, st_k, st_r,
    lb, lt, cb, ct, mf, mt, kb, kt, rf, rt,
    g1_, g6_, g8_, gk_, gx_, send_, obuf_, xbuf_, in1_, in1k_, part_, in2_, in2k_,
    xred_, xroot_, zbuf_, zsum_, mx_, acc, solved2_, solved1_,
    ld, ss_, rs_, fs_, fr_,
):
    leaf = lax.axis_index("leaf")
    me = lax.axis_index("front")
    h = lax.rem(leaf, 2)
    level = lax.div(leaf, 2)
    partner = (leaf + 1 - 2 * h, me)
    across = (lax.rem(leaf + 2, 4), me)
    my_x = lax.rem(me, 4)
    my_z = lax.rem(lax.div(me, 4), 4)
    my_y = lax.div(me, 16)
    line = (my_z, my_x)
    spot = (my_y * 4 + my_x, my_y * 4 + my_z)

    def on_line(way, i):
        return (leaf, my_y * 16 + (i * 4 + my_x if way == 0 else my_z * 4 + i))

    def in_plane(way, u):
        y, other = lax.div(u, 4), lax.rem(u, 4)
        return (leaf, y * 16 + (my_z * 4 + other if way == 0 else other * 4 + my_x))

    def along(way, d):
        return lax.rem(line[way] + d, 4)

    def around(way, d):
        return lax.rem(spot[way] + d, 8)

    def rcopy(src, dst, s, r, dev):
        return pltpu.make_async_remote_copy(
            src_ref=src, dst_ref=dst, send_sem=s, recv_sem=r, device_id=dev, device_id_type=MESH
        )

    def load_columns(src, dst, sem):
        def step(b, c):
            cols = pl.ds(pl.multiple_of(b * 128, 128), 128)
            pltpu.make_async_copy(src.at[:, :, cols], dst.at[b], sem).start()
            return c

        lax.fori_loop(0, dst.shape[0], step, 0)

    def loaded(dst, sem):
        pltpu.make_async_copy(dst, dst, sem).wait()

    load_columns(leaf_inv, st_l, ld.at[0])
    load_columns(leaf_cpl, st_c, ld.at[1])
    pltpu.make_async_copy(mid_inv, st_m, ld.at[2]).start()
    load_columns(mid_cpl, st_k, ld.at[3])
    pltpu.make_async_copy(root_inv, st_r, ld.at[4]).start()

    barrier = pltpu.get_barrier_semaphore()

    def greet(dev):
        pl.semaphore_signal(barrier, 1, device_id=dev, device_id_type=MESH)

    for d in range(8):
        for way in range(2):
            if d % 4 or way == 0:
                dev = in_plane(way, around(way, d))
                greet((across[0], dev[1]))
                if d:
                    greet(dev)
    greet(partner)
    greet((across[0] + partner[0] - leaf, me))
    pl.semaphore_wait(barrier, 29)

    def split_columns(st, b_ref, t_ref):
        def step(q, c):
            for i in range(4):
                b = 4 * q + i
                t = st[b].reshape(128, 128)
                hi, lo = halves(t)
                b_ref[b, 0:128, :] = hi
                b_ref[b, 128:256, :] = lo
                hi, lo = halves(t.T)
                t_ref[b, :, 0:128] = hi
                t_ref[b, :, 128:256] = lo
            return c

        lax.fori_loop(0, st.shape[0] // 4, step, 0)

    def split_rows(st, f_ref, t_ref, n):
        def step(b, c):
            rows = pl.ds(pl.multiple_of(b * 128, 128), 128)
            for part in range(2):
                t = st[part, rows, :]
                hi, lo = halves(t)
                f_ref[b, :, part * n : (part + 1) * n] = hi
                f_ref[b, :, (2 + part) * n : (3 + part) * n] = lo
                hi, lo = halves(t.T)
                t_ref[b, part * n : (part + 1) * n, :] = hi
                t_ref[b, (2 + part) * n : (3 + part) * n, :] = lo
            return c

        lax.fori_loop(0, 16, step, 0)

    def chain(batch):
        g1, g6, g8, gk, gx = (r.at[batch] for r in (g1_, g6_, g8_, gk_, gx_))
        send, obuf, xbuf, in1, in1k = (r.at[batch] for r in (send_, obuf_, xbuf_, in1_, in1k_))
        part, xred, xroot = (r.at[batch] for r in (part_, xred_, xroot_))
        zbuf, zsum, mx, in2k = (r.at[batch] for r in (zbuf_, zsum_, mx_, in2k_))
        solved2, solved1 = solved2_.at[batch], solved1_.at[batch]
        ss, rs, fs, fr = (r.at[batch] for r in (ss_, rs_, fs_, fr_))
        part16 = part.at[:, :, pl.ds(0, 16)]

        def wait_send(some, k):
            rcopy(some, some, ss.at[k], rs.at[k], partner).wait_send()

        def wait_recv(some, k):
            rcopy(some, some, ss.at[k], rs.at[k], partner).wait_recv()

        def three(buf, way):
            return buf.at[way, pl.ds(0, 3)]

        def all_but_one(buf, way):
            return buf.at[way, pl.ds(0, buf.shape[1] - 1)]

        def sum_send(way, d, out, into, k):
            to = along(way, d)
            rcopy(
                out.at[way, to], into.at[way, line[way]], ss.at[k + way], rs.at[k + way], on_line(way, to)
            ).start()

        def sum_own(out, into):
            for way in range(2):
                into[way, line[way]] = out[way, line[way]]

        def sum_second(into, part, into2, k, both=False):
            for way in range(2):
                wait_recv(three(into, way), k + way)
            at = [8 * level + spot[way] if both else spot[way] for way in range(2)]
            for way in range(2):
                part[way] = jnp.sum(into[way], axis=0)
                into2[way, at[way]] = part[way, spot[way]]
            for way in range(2):
                slot = into2.at[way, at[way]]
                sems = ss.at[k + 2 + way], rs.at[k + 2 + way]
                if both:
                    for d in range(8):
                        u = around(way, d)
                        rcopy(part.at[way, u], slot, *sems, (across[0], in_plane(way, u)[1])).start()
                for d in range(1, 8):
                    u = around(way, d)
                    rcopy(part.at[way, u], slot, *sems, in_plane(way, u)).start()

        def sum_last(into2, k):
            for way in range(2):
                wait_recv(all_but_one(into2, way), k + 2 + way)
            return jnp.concatenate([jnp.sum(into2[0], axis=0), jnp.sum(into2[1], axis=0)], axis=0)

        def sum_sent(into, into2, k):
            for way in range(2):
                wait_send(three(into, way), k + way)
                wait_send(all_but_one(into2, way), k + 2 + way)

        def share_first(rows, g, k):
            n = rows.shape[0] // 2
            for way in range(2):
                g[way, line[way], spot[way]] = rows[way * n : (way + 1) * n]
                mine = g.at[way, line[way], spot[way]]
                for d in range(1, 8):
                    u = around(way, d)
                    rcopy(mine, mine, ss.at[k + way], rs.at[k + way], in_plane(way, u)).start()

        def share_second(g, k):
            for way in range(2):
                wait_recv(g.at[way, 0, pl.ds(0, 7)], k + way)
                mine = g.at[way, line[way]]
                for d in range(1, 4):
                    to = on_line(way, along(way, d))
                    rcopy(mine, mine, ss.at[k + 2 + way], rs.at[k + 2 + way], to).start()

        def share_last(g, k):
            for way in range(2):
                wait_recv(three(g, way), k + 2 + way)

        def share_sent(g, k):
            for way in range(2):
                wait_send(g.at[way, 0, pl.ds(0, 7)], k + way)
                wait_send(three(g, way), k + 2 + way)

        def rows_of(g):
            rows = []
            for j in range(NF):
                y, z, x = j // 16, j // 4 % 4, j % 4
                rows += [g[0, z, y * 4 + x], g[1, x, y * 4 + z]]
            return pair(spread(jnp.concatenate(rows, axis=0)))

        def lift_exchange(o_ref, x_ref, way, i, k):
            at = 4 * way + i
            return rcopy(o_ref.at[1 - h, way, i], x_ref.at[way, i], fs.at[k + at], fr.at[k + at], partner)

        def lift(x, t_ref, blocks_of, o_ref, x_ref, subs, k, into, phase):
            rhs = stacked(x)
            n = o_ref.shape[4]
            wide = 8 // subs
            mine = o_ref.at[h]

            def finish(way, d):
                i = along(way, d)
                lift_exchange(o_ref, x_ref, way, i, k).wait_recv()
                mine[way, i] = mine[way, i] + x_ref[way, i]

                @pl.when(d < 4)
                def _():
                    sum_send(way, d, mine, into, phase)

            def step(d, c):
                z = along(0, d)

                def sub(s, c):
                    u = s * wide
                    y, x0 = lax.div(u, 4), lax.rem(u, 4)
                    j = y * 16 + z * 4 + x0
                    lhs = jnp.concatenate([t_ref[b] for b in blocks_of(j)], axis=0)
                    out = squeeze(fold(dot(lhs, rhs))).reshape(wide, 2, 2 * n, 128)
                    for i in range(wide):
                        for side in range(2):
                            o_ref[side, 0, z, u + i] = out[i, side, 0:n]
                            o_ref[side, 1, x0 + i, y * 4 + z] = out[i, side, n : 2 * n]
                    return c

                lax.fori_loop(0, subs, sub, 0)
                lift_exchange(o_ref, x_ref, 0, z, k).start()

                @pl.when(d > 1)
                def _():
                    finish(0, d - 1)

                return c

            lax.fori_loop(1, 5, step, 0)

            def second(d, c):
                lift_exchange(o_ref, x_ref, 1, along(1, d), k).start()
                return c

            lax.fori_loop(1, 5, second, 0)
            finish(0, 4)

            def third(d, c):
                finish(1, d)
                return c

            lax.fori_loop(1, 5, third, 0)
            sum_own(mine, into)
            for way in range(2):
                for i in range(4):
                    lift_exchange(o_ref, x_ref, way, i, k).wait_send()

        def apply(x, f_ref, into, phase):
            rhs = stacked(x)

            def step(d, c):
                z = along(0, d)
                lhs = jnp.concatenate([f_ref[8 * y + 2 * z + i] for y in range(2) for i in range(2)], axis=0)
                out = squeeze(fold(dot(lhs, rhs))).reshape(8, 32, 128)
                send[0, z] = out[:, 0:16]
                for u in range(8):
                    send[1, u % 4, u // 4 * 4 + z] = out[u, 16:32]

                @pl.when(d < 4)
                def _():
                    sum_send(0, d, send, into, phase)

                return c

            lax.fori_loop(1, 5, step, 0)
            for d in range(1, 4):
                sum_send(1, d, send, into, phase)
            sum_own(send, into)

        def forward(g_ref, side, way, i, k):
            at = k + 4 * way + i
            return rcopy(g_ref.at[side, way, i], g_ref.at[side, way, i], fs.at[at], fr.at[at], partner)

        def forward_own(g_ref, k):
            for way in range(2):
                forward(g_ref, h, way, line[way], k).start()

        def forward_rest(g_ref, k):
            for way in range(2):
                for d in range(1, 4):
                    forward(g_ref, h, way, along(way, d), k).start()

        def gather_use(g_ref, blocks_of, b_ref, k):
            for way in range(2):
                for i in range(4):
                    forward(g_ref, 1 - h, way, i, k).wait_recv()
            acc[0:256, :] = jnp.zeros((256, 128), F32)

            def step(z, c):
                lhs, rows = [], []
                for u in range(8):
                    y, x = u // 4, u % 4
                    lhs += [b_ref[b] for b in blocks_of(y * 16 + z * 4 + x)]
                    for side in range(2):
                        rows += [g_ref[side, 0, z, u], g_ref[side, 1, x, y * 4 + z]]
                rhs = pair(spread(jnp.concatenate(rows, axis=0)))
                acc[0:256, :] += dot(jnp.concatenate(lhs, axis=1), rhs)
                return c

            lax.fori_loop(0, 4, step, 0)
            for way in range(2):
                for i in range(4):
                    forward(g_ref, h, way, i, k).wait_send()
            return combine(acc[0:256, :], 64)

        def swap(src, dst, k, dev):
            copy = rcopy(src, dst, ss.at[k], rs.at[k], dev)
            copy.start()
            return copy

        share_first(squeeze(pick(leaf_src[...], batch)), g1, 0)
        yield
        share_second(g1, 0)
        yield
        share_last(g1, 0)
        lhs = jnp.concatenate([lb[b] for b in range(16)], axis=1)
        x = combine(dot(lhs, rows_of(g1)), 64)
        solved2[...] = x
        obuf2 = obuf.at[:, :, :, :, pl.ds(0, 16)]
        xbuf2 = xbuf.at[:, :, :, pl.ds(0, 16)]
        in2 = in2_.at[batch, 0]
        lift(x, ct, lambda j: [inv_two[0, j + i] for i in range(4)], obuf2, xbuf2, 2, 0, in1, 4)
        yield
        sum_second(in1, part16, in2, 4)
        yield
        xred[h] = squeeze(pick(mid_src[...], batch)) - sum_last(in2, 4)
        copy = swap(xred.at[h], xred.at[h], 40, partner)
        copy.wait()
        in2 = in2_.at[batch, 1]
        apply(spread(xred[...].reshape(64, 128)), mf, in1, 8)
        yield
        sum_sent(in1, in2, 4)
        sum_second(in1, part16, in2, 8)
        yield
        x = spread(sum_last(in2, 8))
        solved1[...] = x
        lift(
            x, kt, lambda j: [inv_one[level, 2 * j + i] for i in range(4)], obuf, xbuf, 4, 8, in1k, 12
        )
        yield
        sum_sent(in1, in2, 8)
        sum_second(in1k, part, in2k, 12, both=True)
        yield
        rows = pl.ds(pl.multiple_of(h * 128, 128), 128)
        xroot[h] = squeeze(pick(root_src[rows, :], batch)) - sum_last(in2k, 12)
        copy = swap(xroot.at[h], xroot.at[h], 42, partner)
        copy.wait()
        in2 = in2_.at[batch, 2]
        apply(spread(xroot[...].reshape(128, 128)), rf, in1, 16)
        yield
        sum_sent(in1k, in2k, 12)
        sum_second(in1, part16, in2, 16)
        yield
        share_first(sum_last(in2, 16), g6, 20)
        yield
        share_second(g6, 20)
        yield
        share_last(g6, 20)
        rhs = rows_of(g6)
        for m in range(2):
            lhs = jnp.concatenate([rt[b, m * 512 : (m + 1) * 512, :] for b in range(16)], axis=1)
            acc[m * 512 : (m + 1) * 512, :] = dot(lhs, rhs)
        zbuf[...] = squeeze(combine(acc[...], 256)).reshape(2, 64, 128)
        zsum[leaf] = zbuf[h]
        for side, dev in ((1 - h, partner), (h, across), (1 - h, (across[0] + partner[0] - leaf, me))):
            rcopy(zbuf.at[side], zsum.at[leaf], ss.at[43], rs.at[43], dev).start()
        yield
        wait_recv(zsum.at[pl.ds(0, 3)], 43)
        share_first(jnp.sum(zsum[...], axis=0), gk.at[h], 24)
        yield
        share_second(gk.at[h], 24)
        forward_own(gk, 16)
        yield
        share_last(gk.at[h], 24)
        forward_rest(gk, 16)
        pulled = gather_use(gk, lambda j: [inv_one[level, 2 * j], inv_one[level, 2 * j + 1]], kb, 16)
        share_first(squeeze(solved1[...] - pulled), g8, 28)
        yield
        share_second(g8, 28)
        yield
        share_last(g8, 28)
        lhs = jnp.concatenate([mt[b] for b in range(16)], axis=1)
        x = combine(dot(lhs, rows_of(g8)), 128)
        mx[0:2] = squeeze(x).reshape(2, 32, 128)
        copy = swap(mx.at[1 - h], mx.at[2], 45, partner)
        copy.wait()
        share_first(mx[h] + mx[2], gx.at[h], 32)
        yield
        share_second(gx.at[h], 32)
        forward_own(gx, 24)
        yield
        share_last(gx.at[h], 32)
        forward_rest(gx, 24)
        pulled = gather_use(gx, lambda j: [inv_two[0, j]], cb, 24)
        sum_sent(in1, in2, 16)
        in2 = in2_.at[batch, 3]
        apply(solved2[...] - pulled, lt, in1, 36)
        yield
        sum_second(in1, part16, in2, 36)
        yield
        solved2[...] = spread(sum_last(in2, 36))
        sum_sent(in1, in2, 36)
        wait_send(zsum.at[pl.ds(0, 3)], 43)
        share_sent(g1, 0)
        share_sent(g6, 20)
        share_sent(gk.at[h], 24)
        share_sent(g8, 28)
        share_sent(gx.at[h], 32)

    def prepare_leaf():
        loaded(st_l, ld.at[0])
        split_columns(st_l, lb, lt)
        loaded(st_c, ld.at[1])
        split_columns(st_c, cb, ct)

    def prepare_mid():
        loaded(st_m, ld.at[2])
        split_rows(st_m, mf, mt, 128)

    def prepare_mid_coupling():
        loaded(st_k, ld.at[3])
        split_columns(st_k, kb, kt)

    def prepare_root():
        loaded(st_r, ld.at[4])
        split_rows(st_r, rf, rt, 256)

    prepare = {0: prepare_leaf, 1: prepare_mid, 2: prepare_mid_coupling, 5: prepare_root}
    batches = [chain(0), chain(1)]
    running, at = True, 0
    while running:
        for solve in batches:
            running = next(solve, True) is None
        prepare.get(at, lambda: None)()
        at += 1
    leaf_out[...] = join(solved2_[0], solved2_[1])

    def own_rows(g):
        halves_of = []
        for side in range(2):
            halves_of += [g[side, way, line[way], spot[way]] for way in range(2)]
        return halves_of

    mid = [spread(jnp.concatenate([gx_[b, h, w, line[w], spot[w]] for w in range(2)], axis=0)) for b in range(2)]
    mid_out[...] = join(*mid)
    root_out[...] = join(*[spread(jnp.concatenate(own_rows(gk_.at[b]), axis=0)) for b in range(2)])


def inverse_order(blocks):
    count = blocks.shape[1]
    ids = jnp.arange(count, dtype=jnp.int32)
    hit = blocks[:, :, None] == ids[None, None, :]
    return jnp.sum(jnp.where(hit, ids[None, :, None], 0), axis=1)


def body(
    leaf_source, mid_source, root_source, leaf_inverse, leaf_coupling, mid_inverse, mid_coupling,
    root_inverse, leaf_blocks, mid_blocks,
):
    vmem = pl.BlockSpec(memory_space=pltpu.VMEM)
    smem = pl.BlockSpec(memory_space=pltpu.SMEM)
    hbm = pl.BlockSpec(memory_space=pl.ANY)
    v = pltpu.VMEM
    dma = pltpu.SemaphoreType.DMA
    leaf_out, mid_out, root_out = pl.pallas_call(
        kernel,
        out_shape=(
            jax.ShapeDtypeStruct((64, 128), F32),
            jax.ShapeDtypeStruct((64, 128), F32),
            jax.ShapeDtypeStruct((256, 128), F32),
        ),
        in_specs=[smem, smem, vmem, vmem, vmem, hbm, hbm, hbm, hbm, hbm],
        out_specs=(vmem, vmem, vmem),
        scratch_shapes=[
            v((16, 2, 64, 128), F32), v((32, 2, 64, 128), F32), v((2, 2048, 128), F32),
            v((64, 2, 64, 128), F32), v((2, 2048, 256), F32),
            v((16, 256, 128), BF16), v((16, 128, 256), BF16),
            v((32, 256, 128), BF16), v((32, 128, 256), BF16),
            v((16, 128, 512), BF16), v((16, 512, 128), BF16),
            v((64, 256, 128), BF16), v((64, 128, 256), BF16),
            v((16, 128, 1024), BF16), v((16, 1024, 128), BF16),
            v((2, 2, 4, 8, 16, 128), F32), v((2, 2, 4, 8, 16, 128), F32), v((2, 2, 4, 8, 16, 128), F32),
            v((2, 2, 2, 4, 8, 32, 128), F32), v((2, 2, 2, 4, 8, 16, 128), F32),
            v((2, 2, 4, 8, 16, 128), F32), v((2, 2, 2, 4, 8, 32, 128), F32), v((2, 2, 4, 8, 32, 128), F32),
            v((2, 2, 4, 8, 16, 128), F32), v((2, 2, 4, 8, 32, 128), F32), v((2, 2, 8, 32, 128), F32),
            v((2, 4, 2, 8, 16, 128), F32), v((2, 2, 16, 32, 128), F32),
            v((2, 2, 32, 128), F32), v((2, 2, 64, 128), F32),
            v((2, 2, 64, 128), F32), v((2, 4, 64, 128), F32), v((2, 3, 32, 128), F32),
            v((1024, 128), F32), v((2, 64, 128), F32), v((2, 64, 128), F32),
            dma((5,)), dma((2, 48)), dma((2, 48)), dma((2, 32)), dma((2, 32)),
        ],
        compiler_params=pltpu.CompilerParams(
            collective_id=0, has_side_effects=True, vmem_limit_bytes=67043328
        ),
    )(
        inverse_order(leaf_blocks), inverse_order(mid_blocks),
        leaf_source[0], mid_source[0], root_source,
        leaf_inverse[0], jnp.swapaxes(leaf_coupling[0], 1, 2), mid_inverse[0],
        jnp.swapaxes(mid_coupling[0], 1, 2), root_inverse,
    )
    return leaf_out[None], mid_out[None], root_out


def solution(mesh):
    placed = (
        P("leaf", "front", None), P("leaf", "front", None), P("front", None),
        P("leaf", None, "front", None), P("leaf", None, None, "front"),
        P("leaf", None, None, "front"), P("leaf", None, None, "front"),
        P(None, "leaf", "front"), P("leaf", None), P(),
    )
    return jax.shard_map(
        body,
        mesh=mesh,
        in_specs=placed,
        out_specs=(P("leaf", "front", None), P("leaf", "front", None), P("front", None)),
        check_vma=False,
    )
```

```python
import jax
import jax.numpy as jnp
from jax import lax
from jax.experimental import pallas as pl
from jax.experimental.pallas import tpu as pltpu
from jax.sharding import PartitionSpec as P

MESH = pl.DeviceIdType.MESH
F32 = jnp.float32
BF16 = jnp.bfloat16
NF = 32


def lanes(x):
    return lax.broadcasted_iota(jnp.int32, x.shape, x.ndim - 1)


def low(x):
    return lanes(x) < 64


def quarter(x):
    return lanes(x) // 32


def pick(x, batch):
    x = pltpu.roll(x, 96, 1) if batch else x
    q = quarter(x)
    upper = jnp.where(q == 2, pltpu.roll(x, 64, 1), pltpu.roll(x, 32, 1))
    return jnp.where(q == 0, x, jnp.where(q == 1, pltpu.roll(x, 96, 1), upper))


def join(a, b):
    q = quarter(a)
    upper = jnp.where(q == 2, pltpu.roll(a, 32, 1), b)
    return jnp.where(q == 0, a, jnp.where(q == 1, pltpu.roll(b, 32, 1), upper))


def squeeze(wide):
    n = wide.shape[0] // 64
    parts = wide.reshape(n, 2, 32, 128)
    first, second = parts[:, 0], parts[:, 1]
    return jnp.where(low(first), first, second).reshape(n * 32, 128)


def spread(packed):
    n = packed.shape[0] // 32
    other = pltpu.roll(packed, 64, 1)
    first = jnp.where(low(packed), packed, other).reshape(n, 32, 128)
    second = jnp.where(low(packed), other, packed).reshape(n, 32, 128)
    return jnp.concatenate([first, second], axis=1).reshape(n * 64, 128)


def halves(x):
    hi = x.astype(BF16)
    lo = (x - hi.astype(F32)).astype(BF16)
    return hi, lo


def pair(wide):
    hi = wide.astype(BF16).astype(F32)
    return jnp.where(low(wide), hi, wide - hi).astype(BF16)


def turn(wide):
    swapped = pltpu.roll(wide, 32, 1)
    return jnp.where(lanes(wide) % 64 < 32, -swapped, swapped)


def stacked(wide):
    both = jnp.concatenate([pair(wide), pair(turn(wide))], axis=0)
    return jnp.concatenate([both, both], axis=0)


def dot(a, b):
    return jnp.dot(a, b, preferred_element_type=F32)


def fold(a):
    return a + pltpu.roll(a, 64, 1)


def combine(a, n):
    folded = fold(a)
    real = folded[:n] + folded[2 * n : 3 * n]
    imag = folded[n : 2 * n] + folded[3 * n :]
    return real + turn(imag)


def kernel(
    orders, leaf_src, mid_src, root_src, leaf_inv, leaf_cpl, mid_inv, mid_cpl, root_inv,
    leaf_out, mid_out, root_out,
    st_l, st_c, st_m, st_k, st_r,
    lb, lt, cb, ct, mf, mt, kb, kt, rf, rt,
    g1_, g6_, g8_, gk_, gx_, send_, obuf_, xbuf_, in1_, in1k_, part_, in2_, in2k_,
    xred_, xroot_, zbuf_, zsum_, mx_, acc, solved2_, solved1_,
    ld, ss_, rs_, fs_, fr_,
):
    leaf = lax.axis_index("leaf")
    me = lax.axis_index("front")
    h = lax.rem(leaf, 2)
    level = lax.div(leaf, 2)
    partner = (leaf + 1 - 2 * h, me)
    across = (lax.rem(leaf + 2, 4), me)
    my_x = lax.rem(me, 4)
    my_z = lax.rem(lax.div(me, 4), 4)
    my_y = lax.div(me, 16)
    line = (my_z, my_x)
    spot = (my_y * 4 + my_x, my_y * 4 + my_z)

    def on_line(way, i):
        return (leaf, my_y * 16 + (i * 4 + my_x if way == 0 else my_z * 4 + i))

    def in_plane(way, u):
        y, other = lax.div(u, 4), lax.rem(u, 4)
        return (leaf, y * 16 + (my_z * 4 + other if way == 0 else other * 4 + my_x))

    def along(way, d):
        return lax.rem(line[way] + d, 4)

    def around(way, d):
        return lax.rem(spot[way] + d, 8)

    def rcopy(src, dst, s, r, dev):
        return pltpu.make_async_remote_copy(
            src_ref=src, dst_ref=dst, send_sem=s, recv_sem=r, device_id=dev, device_id_type=MESH
        )

    def load_columns(src, dst, sem):
        def step(b, c):
            cols = pl.ds(pl.multiple_of(b * 128, 128), 128)
            pltpu.make_async_copy(src.at[:, :, cols], dst.at[b], sem).start()
            return c

        lax.fori_loop(0, dst.shape[0], step, 0)

    def loaded(dst, sem):
        pltpu.make_async_copy(dst, dst, sem).wait()

    barrier = pltpu.get_barrier_semaphore()

    def greet(dev):
        pl.semaphore_signal(barrier, 1, device_id=dev, device_id_type=MESH)

    for d in range(8):
        for way in range(2):
            if d % 4 or way == 0:
                dev = in_plane(way, around(way, d))
                greet((across[0], dev[1]))
                if d:
                    greet(dev)
    greet(partner)
    greet((across[0] + partner[0] - leaf, me))
    load_columns(leaf_inv, st_l, ld.at[0])
    load_columns(leaf_cpl, st_c, ld.at[1])
    pl.semaphore_wait(barrier, 29)

    def split_columns(st, b_ref, t_ref):
        def step(q, c):
            for i in range(4):
                b = 4 * q + i
                t = st[b].reshape(128, 128)
                hi, lo = halves(t)
                b_ref[b, 0:128, :] = hi
                b_ref[b, 128:256, :] = lo
                hi, lo = halves(t.T)
                t_ref[b, :, 0:128] = hi
                t_ref[b, :, 128:256] = lo
            return c

        lax.fori_loop(0, st.shape[0] // 4, step, 0)

    def split_rows(st, f_ref, t_ref, n):
        def step(b, c):
            rows = pl.ds(pl.multiple_of(b * 128, 128), 128)
            for part in range(2):
                t = st[part, rows, :]
                hi, lo = halves(t)
                f_ref[b, :, part * n : (part + 1) * n] = hi
                f_ref[b, :, (2 + part) * n : (3 + part) * n] = lo
                hi, lo = halves(t.T)
                t_ref[b, part * n : (part + 1) * n, :] = hi
                t_ref[b, (2 + part) * n : (3 + part) * n, :] = lo
            return c

        lax.fori_loop(0, 16, step, 0)

    def chain(batch):
        g1, g6, g8, gk, gx = (r.at[batch] for r in (g1_, g6_, g8_, gk_, gx_))
        send, obuf, xbuf, in1, in1k = (r.at[batch] for r in (send_, obuf_, xbuf_, in1_, in1k_))
        part, xred, xroot = (r.at[batch] for r in (part_, xred_, xroot_))
        zbuf, zsum, mx, in2k = (r.at[batch] for r in (zbuf_, zsum_, mx_, in2k_))
        solved2, solved1 = solved2_.at[batch], solved1_.at[batch]
        ss, rs, fs, fr = (r.at[batch] for r in (ss_, rs_, fs_, fr_))
        part16 = part.at[:, :, pl.ds(0, 16)]

        def wait_send(some, k):
            rcopy(some, some, ss.at[k], rs.at[k], partner).wait_send()

        def wait_recv(some, k):
            rcopy(some, some, ss.at[k], rs.at[k], partner).wait_recv()

        def three(buf, way):
            return buf.at[way, pl.ds(0, 3)]

        def all_but_one(buf, way):
            return buf.at[way, pl.ds(0, buf.shape[1] - 1)]

        def sum_send(way, d, out, into, k):
            to = along(way, d)
            rcopy(
                out.at[way, to], into.at[way, line[way]], ss.at[k + way], rs.at[k + way], on_line(way, to)
            ).start()

        def sum_own(out, into):
            for way in range(2):
                into[way, line[way]] = out[way, line[way]]

        def sum_second(into, part, into2, k, both=False):
            for way in range(2):
                wait_recv(three(into, way), k + way)
            at = [8 * level + spot[way] if both else spot[way] for way in range(2)]
            for way in range(2):
                part[way] = jnp.sum(into[way], axis=0)
                into2[way, at[way]] = part[way, spot[way]]
            for way in range(2):
                slot = into2.at[way, at[way]]
                sems = ss.at[k + 2 + way], rs.at[k + 2 + way]
                if both:
                    for d in range(8):
                        u = around(way, d)
                        rcopy(part.at[way, u], slot, *sems, (across[0], in_plane(way, u)[1])).start()
                for d in range(1, 8):
                    u = around(way, d)
                    rcopy(part.at[way, u], slot, *sems, in_plane(way, u)).start()

        def sum_last(into2, k):
            for way in range(2):
                wait_recv(all_but_one(into2, way), k + 2 + way)
            return jnp.concatenate([jnp.sum(into2[0], axis=0), jnp.sum(into2[1], axis=0)], axis=0)

        def sum_sent(into, into2, k):
            for way in range(2):
                wait_send(three(into, way), k + way)
                wait_send(all_but_one(into2, way), k + 2 + way)

        def share_first(rows, g, k):
            n = rows.shape[0] // 2
            for way in range(2):
                g[way, line[way], spot[way]] = rows[way * n : (way + 1) * n]
                mine = g.at[way, line[way], spot[way]]
                for d in range(1, 8):
                    u = around(way, d)
                    rcopy(mine, mine, ss.at[k + way], rs.at[k + way], in_plane(way, u)).start()

        def share_second(g, k):
            for way in range(2):
                wait_recv(g.at[way, 0, pl.ds(0, 7)], k + way)
                mine = g.at[way, line[way]]
                for d in range(1, 4):
                    to = on_line(way, along(way, d))
                    rcopy(mine, mine, ss.at[k + 2 + way], rs.at[k + 2 + way], to).start()

        def share_last(g, k):
            for way in range(2):
                wait_recv(three(g, way), k + 2 + way)

        def share_sent(g, k):
            for way in range(2):
                wait_send(g.at[way, 0, pl.ds(0, 7)], k + way)
                wait_send(three(g, way), k + 2 + way)

        def rows_of(g):
            rows = []
            for j in range(NF):
                y, z, x = j // 16, j // 4 % 4, j % 4
                rows += [g[0, z, y * 4 + x], g[1, x, y * 4 + z]]
            return pair(spread(jnp.concatenate(rows, axis=0)))

        def lift_exchange(o_ref, x_ref, way, i, k):
            at = 4 * way + i
            return rcopy(o_ref.at[1 - h, way, i], x_ref.at[way, i], fs.at[k + at], fr.at[k + at], partner)

        def lift(x, t_ref, blocks_of, o_ref, x_ref, subs, k, into, phase):
            rhs = stacked(x)
            n = o_ref.shape[4]
            wide = 8 // subs
            mine = o_ref.at[h]

            def finish(way, d):
                i = along(way, d)
                lift_exchange(o_ref, x_ref, way, i, k).wait_recv()
                mine[way, i] = mine[way, i] + x_ref[way, i]

                @pl.when(d < 4)
                def _():
                    sum_send(way, d, mine, into, phase)

            def step(d, c):
                z = along(0, d)

                def sub(s, c):
                    u = s * wide
                    y, x0 = lax.div(u, 4), lax.rem(u, 4)
                    j = y * 16 + z * 4 + x0
                    lhs = jnp.concatenate([t_ref[b] for b in blocks_of(j)], axis=0)
                    out = squeeze(fold(dot(lhs, rhs))).reshape(wide, 2, 2 * n, 128)
                    for i in range(wide):
                        for side in range(2):
                            o_ref[side, 0, z, u + i] = out[i, side, 0:n]
                            o_ref[side, 1, x0 + i, y * 4 + z] = out[i, side, n : 2 * n]
                    return c

                lax.fori_loop(0, subs, sub, 0)
                lift_exchange(o_ref, x_ref, 0, z, k).start()

                @pl.when(d > 1)
                def _():
                    finish(0, d - 1)

                return c

            lax.fori_loop(1, 5, step, 0)

            def second(d, c):
                lift_exchange(o_ref, x_ref, 1, along(1, d), k).start()
                return c

            lax.fori_loop(1, 5, second, 0)
            finish(0, 4)

            def third(d, c):
                finish(1, d)
                return c

            lax.fori_loop(1, 5, third, 0)
            sum_own(mine, into)
            for way in range(2):
                for i in range(4):
                    lift_exchange(o_ref, x_ref, way, i, k).wait_send()

        def apply(x, f_ref, into, phase):
            rhs = stacked(x)

            def step(d, c):
                z = along(0, d)
                lhs = jnp.concatenate([f_ref[8 * y + 2 * z + i] for y in range(2) for i in range(2)], axis=0)
                out = squeeze(fold(dot(lhs, rhs))).reshape(8, 32, 128)
                send[0, z] = out[:, 0:16]
                for u in range(8):
                    send[1, u % 4, u // 4 * 4 + z] = out[u, 16:32]

                @pl.when(d < 4)
                def _():
                    sum_send(0, d, send, into, phase)

                return c

            lax.fori_loop(1, 5, step, 0)
            for d in range(1, 4):
                sum_send(1, d, send, into, phase)
            sum_own(send, into)

        def forward(g_ref, side, way, i, k):
            at = k + 4 * way + i
            return rcopy(g_ref.at[side, way, i], g_ref.at[side, way, i], fs.at[at], fr.at[at], partner)

        def forward_own(g_ref, k):
            for way in range(2):
                forward(g_ref, h, way, line[way], k).start()

        def forward_rest(g_ref, k):
            for way in range(2):
                for d in range(1, 4):
                    forward(g_ref, h, way, along(way, d), k).start()

        def gather_use(g_ref, blocks_of, b_ref, k):
            for way in range(2):
                for i in range(4):
                    forward(g_ref, 1 - h, way, i, k).wait_recv()
            acc[0:256, :] = jnp.zeros((256, 128), F32)

            def step(z, c):
                lhs, rows = [], []
                for u in range(8):
                    y, x = u // 4, u % 4
                    lhs += [b_ref[b] for b in blocks_of(y * 16 + z * 4 + x)]
                    for side in range(2):
                        rows += [g_ref[side, 0, z, u], g_ref[side, 1, x, y * 4 + z]]
                rhs = pair(spread(jnp.concatenate(rows, axis=0)))
                acc[0:256, :] += dot(jnp.concatenate(lhs, axis=1), rhs)
                return c

            lax.fori_loop(0, 4, step, 0)
            for way in range(2):
                for i in range(4):
                    forward(g_ref, h, way, i, k).wait_send()
            return combine(acc[0:256, :], 64)

        def swap(src, dst, k, dev):
            copy = rcopy(src, dst, ss.at[k], rs.at[k], dev)
            copy.start()
            return copy

        share_first(squeeze(pick(leaf_src[...], batch)), g1, 0)
        yield
        share_second(g1, 0)
        yield
        share_last(g1, 0)
        lhs = jnp.concatenate([lb[b] for b in range(16)], axis=1)
        x = combine(dot(lhs, rows_of(g1)), 64)
        solved2[...] = x
        obuf2 = obuf.at[:, :, :, :, pl.ds(0, 16)]
        xbuf2 = xbuf.at[:, :, :, pl.ds(0, 16)]
        in2 = in2_.at[batch, 0]
        lift(x, ct, lambda j: [orders[2, j + i] for i in range(4)], obuf2, xbuf2, 2, 0, in1, 4)
        yield
        sum_second(in1, part16, in2, 4)
        yield
        xred[h] = squeeze(pick(mid_src[...], batch)) - sum_last(in2, 4)
        copy = swap(xred.at[h], xred.at[h], 40, partner)
        copy.wait()
        in2 = in2_.at[batch, 1]
        apply(spread(xred[...].reshape(64, 128)), mf, in1, 8)
        yield
        sum_sent(in1, in2, 4)
        sum_second(in1, part16, in2, 8)
        yield
        x = spread(sum_last(in2, 8))
        solved1[...] = x
        lift(
            x, kt, lambda j: [orders[level, 2 * j + i] for i in range(4)], obuf, xbuf, 4, 8, in1k, 12
        )
        yield
        sum_sent(in1, in2, 8)
        sum_second(in1k, part, in2k, 12, both=True)
        yield
        rows = pl.ds(pl.multiple_of(h * 128, 128), 128)
        xroot[h] = squeeze(pick(root_src[rows, :], batch)) - sum_last(in2k, 12)
        copy = swap(xroot.at[h], xroot.at[h], 42, partner)
        copy.wait()
        in2 = in2_.at[batch, 2]
        apply(spread(xroot[...].reshape(128, 128)), rf, in1, 16)
        yield
        sum_sent(in1k, in2k, 12)
        sum_second(in1, part16, in2, 16)
        yield
        share_first(sum_last(in2, 16), g6, 20)
        yield
        share_second(g6, 20)
        yield
        share_last(g6, 20)
        rhs = rows_of(g6)
        for m in range(2):
            lhs = jnp.concatenate([rt[b, m * 512 : (m + 1) * 512, :] for b in range(16)], axis=1)
            acc[m * 512 : (m + 1) * 512, :] = dot(lhs, rhs)
        zbuf[...] = squeeze(combine(acc[...], 256)).reshape(2, 64, 128)
        zsum[leaf] = zbuf[h]
        for side, dev in ((1 - h, partner), (h, across), (1 - h, (across[0] + partner[0] - leaf, me))):
            rcopy(zbuf.at[side], zsum.at[leaf], ss.at[43], rs.at[43], dev).start()
        yield
        wait_recv(zsum.at[pl.ds(0, 3)], 43)
        share_first(jnp.sum(zsum[...], axis=0), gk.at[h], 24)
        yield
        share_second(gk.at[h], 24)
        forward_own(gk, 16)
        yield
        share_last(gk.at[h], 24)
        forward_rest(gk, 16)
        pulled = gather_use(gk, lambda j: [orders[level, 2 * j], orders[level, 2 * j + 1]], kb, 16)
        share_first(squeeze(solved1[...] - pulled), g8, 28)
        yield
        share_second(g8, 28)
        yield
        share_last(g8, 28)
        lhs = jnp.concatenate([mt[b] for b in range(16)], axis=1)
        x = combine(dot(lhs, rows_of(g8)), 128)
        mx[0:2] = squeeze(x).reshape(2, 32, 128)
        copy = swap(mx.at[1 - h], mx.at[2], 45, partner)
        copy.wait()
        share_first(mx[h] + mx[2], gx.at[h], 32)
        yield
        share_second(gx.at[h], 32)
        forward_own(gx, 24)
        yield
        share_last(gx.at[h], 32)
        forward_rest(gx, 24)
        pulled = gather_use(gx, lambda j: [orders[2, j]], cb, 24)
        sum_sent(in1, in2, 16)
        in2 = in2_.at[batch, 3]
        apply(solved2[...] - pulled, lt, in1, 36)
        yield
        sum_second(in1, part16, in2, 36)
        yield
        solved2[...] = spread(sum_last(in2, 36))
        sum_sent(in1, in2, 36)
        wait_send(zsum.at[pl.ds(0, 3)], 43)
        share_sent(g1, 0)
        share_sent(g6, 20)
        share_sent(gk.at[h], 24)
        share_sent(g8, 28)
        share_sent(gx.at[h], 32)

    def prepare_leaf():
        pltpu.make_async_copy(mid_inv, st_m, ld.at[2]).start()
        load_columns(mid_cpl, st_k, ld.at[3])
        pltpu.make_async_copy(root_inv, st_r, ld.at[4]).start()
        loaded(st_l, ld.at[0])
        split_columns(st_l, lb, lt)
        loaded(st_c, ld.at[1])
        split_columns(st_c, cb, ct)

    def prepare_mid():
        loaded(st_m, ld.at[2])
        split_rows(st_m, mf, mt, 128)

    def prepare_mid_coupling():
        loaded(st_k, ld.at[3])
        split_columns(st_k, kb, kt)

    def prepare_root():
        loaded(st_r, ld.at[4])
        split_rows(st_r, rf, rt, 256)

    prepare = {0: prepare_leaf, 1: prepare_mid, 2: prepare_mid_coupling, 5: prepare_root}
    batches = [chain(0), chain(1)]
    running, at = True, 0
    while running:
        for solve in batches:
            running = next(solve, True) is None
        prepare.get(at, lambda: None)()
        at += 1
    leaf_out[...] = join(solved2_[0], solved2_[1])

    def own_rows(g):
        halves_of = []
        for side in range(2):
            halves_of += [g[side, way, line[way], spot[way]] for way in range(2)]
        return halves_of

    mid = [spread(jnp.concatenate([gx_[b, h, w, line[w], spot[w]] for w in range(2)], axis=0)) for b in range(2)]
    mid_out[...] = join(*mid)
    root_out[...] = join(*[spread(jnp.concatenate(own_rows(gk_.at[b]), axis=0)) for b in range(2)])


def inverse_order(blocks):
    count = blocks.shape[1]
    ids = jnp.arange(count, dtype=jnp.int32)
    hit = blocks[:, :, None] == ids[None, None, :]
    return jnp.sum(jnp.where(hit, ids[None, :, None], 0), axis=1)


def hand_over(leaf_in, mid_in, root_in, leaf_out, mid_out, root_out):
    leaf_out[...] = leaf_in[...]
    mid_out[...] = mid_in[...]
    root_out[...] = root_in[...]


def body(
    leaf_source, mid_source, root_source, leaf_inverse, leaf_coupling, mid_inverse, mid_coupling,
    root_inverse, leaf_blocks, mid_blocks,
):
    vmem = pl.BlockSpec(memory_space=pltpu.VMEM)
    smem = pl.BlockSpec(memory_space=pltpu.SMEM)
    hbm = pl.BlockSpec(memory_space=pl.ANY)
    v = pltpu.VMEM
    dma = pltpu.SemaphoreType.DMA
    leaf_out, mid_out, root_out = pl.pallas_call(
        kernel,
        out_shape=(
            jax.ShapeDtypeStruct((64, 128), F32),
            jax.ShapeDtypeStruct((64, 128), F32),
            jax.ShapeDtypeStruct((256, 128), F32),
        ),
        in_specs=[smem, vmem, vmem, vmem, hbm, hbm, hbm, hbm, hbm],
        out_specs=(vmem, vmem, vmem),
        scratch_shapes=[
            v((16, 2, 64, 128), F32), v((32, 2, 64, 128), F32), v((2, 2048, 128), F32),
            v((64, 2, 64, 128), F32), v((2, 2048, 256), F32),
            v((16, 256, 128), BF16), v((16, 128, 256), BF16),
            v((32, 256, 128), BF16), v((32, 128, 256), BF16),
            v((16, 128, 512), BF16), v((16, 512, 128), BF16),
            v((64, 256, 128), BF16), v((64, 128, 256), BF16),
            v((16, 128, 1024), BF16), v((16, 1024, 128), BF16),
            v((2, 2, 4, 8, 16, 128), F32), v((2, 2, 4, 8, 16, 128), F32), v((2, 2, 4, 8, 16, 128), F32),
            v((2, 2, 2, 4, 8, 32, 128), F32), v((2, 2, 2, 4, 8, 16, 128), F32),
            v((2, 2, 4, 8, 16, 128), F32), v((2, 2, 2, 4, 8, 32, 128), F32), v((2, 2, 4, 8, 32, 128), F32),
            v((2, 2, 4, 8, 16, 128), F32), v((2, 2, 4, 8, 32, 128), F32), v((2, 2, 8, 32, 128), F32),
            v((2, 4, 2, 8, 16, 128), F32), v((2, 2, 16, 32, 128), F32),
            v((2, 2, 32, 128), F32), v((2, 2, 64, 128), F32),
            v((2, 2, 64, 128), F32), v((2, 4, 64, 128), F32), v((2, 3, 32, 128), F32),
            v((1024, 128), F32), v((2, 64, 128), F32), v((2, 64, 128), F32),
            dma((5,)), dma((2, 48)), dma((2, 48)), dma((2, 32)), dma((2, 32)),
        ],
        compiler_params=pltpu.CompilerParams(
            collective_id=0, has_side_effects=True, vmem_limit_bytes=67043328
        ),
    )(
        inverse_order(jnp.concatenate([mid_blocks, jnp.pad(leaf_blocks, ((0, 0), (0, 32)), constant_values=-1)])),
        leaf_source[0], mid_source[0], root_source,
        leaf_inverse[0], jnp.swapaxes(leaf_coupling[0], 1, 2), mid_inverse[0],
        jnp.swapaxes(mid_coupling[0], 1, 2), root_inverse,
    )
    leaf_out, mid_out, root_out = pl.pallas_call(
        hand_over,
        out_shape=(
            jax.ShapeDtypeStruct((64, 128), F32),
            jax.ShapeDtypeStruct((64, 128), F32),
            jax.ShapeDtypeStruct((256, 128), F32),
        ),
        in_specs=[vmem, vmem, vmem],
        out_specs=(vmem, vmem, vmem),
    )(leaf_out, mid_out, root_out)
    return leaf_out[None], mid_out[None], root_out


def solution(mesh):
    placed = (
        P("leaf", "front", None), P("leaf", "front", None), P("front", None),
        P("leaf", None, "front", None), P("leaf", None, None, "front"),
        P("leaf", None, None, "front"), P("leaf", None, None, "front"),
        P(None, "leaf", "front"), P("leaf", None), P(),
    )
    return jax.shard_map(
        body,
        mesh=mesh,
        in_specs=placed,
        out_specs=(P("leaf", "front", None), P("leaf", "front", None), P("front", None)),
        check_vma=False,
    )
```
